512 devices in a mesh: seq: 128 (over y, z_hi, x), head: 4 (over z_lo, core).
Axes of the slice: x: 4, y: 8, z: 8 (z_hi: 4, z_lo: 2; z = z_hi * 2 + z_lo), core: 2. Of those that a mesh axis runs over, the one named last changes fastest.
Arguments:
- fixed_point: bfloat16 [16384, 2048], P('seq'), may hold values from -7 to 7
- upstream: bfloat16 [16384, 2048], P('seq'), may hold values from -70 to 70
- norm_gain: float32 [2048], replicated, may hold values from 0.7 to 1.3
- query_weight: bfloat16 [2048, 1024], P(None, 'head'), may hold values from -0.35355339 to 0.35355339
- keyval_weight: bfloat16 [2048, 512], P(None, 'head'), may hold values from -0.143631065 to 0.143631065
- output_weight: bfloat16 [1024, 2048], P('head'), may hold values from -0.09375 to 0.09375
- log_norm: float32 [16, 16384], P('head', 'seq'), as said below
- attention_out: bfloat16 [16384, 1024], P('seq', 'head'), as said below
Outputs:
- adjoint: float32 [16384, 2048], P('seq')
The draws below stay inside these ranges and needn't reach their ends.
Inputs may be any that keep to these rules, and one draw needn't show every extreme that they name: log_norm[h, t] is the log of the sum over the keys that query t sees of exp(scores[h, t, j]), with scores computed from fixed_point, norm_gain, query_weight and keyval_weight as in the reference program. attention_out[t, h] is the sum over the keys that query t sees of exp(scores[h, t, j] - log_norm[h, t]) v_c(j), rounded to bfloat16.
All inputs are finite; a program needn't handle non-finite values.
Results may differ from the reference program's by a relative error of at most 0.012.
The reference program's roundings to bfloat16 on the way count: a program that leaves them out, or rounds other values in their place, can miss the bound.
Values may be sent and summed in bfloat16 or wider, within the bound.
A program may use at most 64 MiB of HBM per device.

```python
import jax
import jax.numpy as jnp
from jax import lax

D = 2048
HEADS = 16
KV_HEADS = 4
HEAD_DIM = 64
TOK_DEV = 128
WIN_DEVS = 4
ITERS = 3
TOKENS = 16384


norm_eps = 1e-05


def layer_draw(key):
    subkeys = jax.random.split(jax.random.fold_in(key, 4099), 5)
    latent = jnp.clip(jax.random.normal(subkeys[0], (TOKENS, D), jnp.float32), -6.0, 6.0)
    gains = 1.0 + 0.15 * jax.random.uniform(subkeys[2], (D,), jnp.float32, -1.0, 1.0)
    query_weight = jnp.clip(jax.random.normal(subkeys[3], (D, HEADS * HEAD_DIM), jnp.float32), -6.0, 6.0) * (2.5 / D ** 0.5)
    keyval_weight = jnp.clip(jax.random.normal(subkeys[4], (D, KV_HEADS * 2 * HEAD_DIM), jnp.float32), -6.0, 6.0) / D ** 0.5
    return (latent.astype(jnp.bfloat16), gains, query_weight.astype(jnp.bfloat16), keyval_weight.astype(jnp.bfloat16))


def window_mask_drawn(block_id):
    key_pos = jnp.arange((WIN_DEVS + 1) * TOK_DEV).astype(jnp.int32)[None, :]
    query_pos = jnp.arange(TOK_DEV).astype(jnp.int32)[:, None]
    lowest = (WIN_DEVS - block_id) * TOK_DEV
    return (key_pos > query_pos) & (key_pos <= query_pos + WIN_DEVS * TOK_DEV) & (key_pos >= lowest)


def window_stats(key):
    latent, gains, query_weight, keyval_weight = layer_draw(key)
    group_size = HEADS // KV_HEADS
    block_total = TOKENS // TOK_DEV
    key_span = (WIN_DEVS + 1) * TOK_DEV
    latent_f = latent.astype(jnp.float32)
    normed = latent_f * lax.rsqrt(jnp.mean(latent_f * latent_f, axis=1, keepdims=True) + norm_eps)
    hidden = (normed * gains).astype(jnp.bfloat16)
    queries = jnp.dot(hidden, query_weight, preferred_element_type=jnp.float32).astype(jnp.bfloat16)
    keyval = jnp.dot(hidden, keyval_weight, preferred_element_type=jnp.float32).astype(jnp.bfloat16)
    padding = jnp.zeros((WIN_DEVS * TOK_DEV, KV_HEADS * 2 * HEAD_DIM), jnp.bfloat16)
    padded = jnp.concatenate([padding, keyval], axis=0)

    def one_block(block_id):
        first_row = block_id * TOK_DEV
        query_blk = lax.dynamic_slice_in_dim(queries, first_row, TOK_DEV, 0).astype(jnp.float32)
        query_blk = query_blk.reshape(TOK_DEV, KV_HEADS, group_size, HEAD_DIM)
        window = lax.dynamic_slice_in_dim(padded, first_row, key_span, 0).astype(jnp.float32)
        window = window.reshape(key_span, KV_HEADS, 2, HEAD_DIM)
        scores = jnp.einsum('rcge,pce->cgrp', query_blk, window[:, :, 0]) * HEAD_DIM ** (-0.5)
        allowed = window_mask_drawn(block_id)
        masked = jnp.where(allowed, scores, -1e+30)
        totals = jax.nn.logsumexp(masked, axis=-1)
        weights_blk = jnp.where(allowed, jnp.exp(scores - totals[..., None]), 0.0)
        outputs = jnp.einsum('cgrp,pce->rcge', weights_blk, window[:, :, 1]).reshape(TOK_DEV, HEADS * HEAD_DIM)
        return (totals.reshape(HEADS, TOK_DEV), outputs)
    totals, outputs = lax.map(one_block, jnp.arange(block_total).astype(jnp.int32))
    log_totals = jnp.transpose(totals, (1, 0, 2)).reshape(HEADS, TOKENS)
    return (log_totals, outputs.reshape(TOKENS, HEADS * HEAD_DIM))


def draw_fixed_point(key, part):
    return layer_draw(key)[0]


def draw_norm_gain(key, part):
    return layer_draw(key)[1]


def draw_query_weight(key, part):
    return layer_draw(key)[2]


def draw_keyval_weight(key, part):
    return layer_draw(key)[3]


def draw_log_norm(key, part):
    return window_stats(key)[0]


def draw_attention_out(key, part):
    return window_stats(key)[1].astype(jnp.bfloat16)


def draw_upstream(key, part):
    subkeys = jax.random.split(jax.random.fold_in(key, 9173), 4)
    position = jnp.arange(TOKENS).astype(jnp.float32)[:, None] / TOKENS
    rising = jnp.exp(jnp.log(3.0) * (position - 0.5))
    row_scale = jnp.exp(jax.random.uniform(subkeys[1], (TOKENS, 1), jnp.float32, -1.15, 1.15))
    column_scale = jnp.exp(jax.random.uniform(subkeys[2], (1, D), jnp.float32, -1.15, 1.15))
    noise_field = jnp.clip(jax.random.normal(subkeys[0], (TOKENS, D), jnp.float32), -4.0, 4.0)
    return (noise_field * rising * row_scale * column_scale).astype(jnp.bfloat16)


def block_levels(own_key, extent, shards, smallest, high):
    def one(dim, blocks):
        draws = jax.random.uniform(jax.random.fold_in(jax.random.fold_in(own_key, 6), dim), (blocks,), jnp.float32, smallest / len(shards), high / len(shards))
        return jnp.repeat(jnp.exp(draws), extent[dim] // blocks).reshape((-1,) + (1,) * (len(extent) - dim - 1))

    level = one(*shards[0])
    for cut in shards[1:]:
        level = level * one(*cut)
    return level


def gaussian(rng, extent, width, bound, pieces=(), dtype=jnp.bfloat16):
    factor_of = block_levels(rng, extent, pieces, -0.22, 0.18) if pieces else 1.0
    result = jax.random.normal(rng, extent, jnp.float32) * width * factor_of
    return jnp.minimum(jnp.maximum(result, -bound), bound).astype(dtype)


def setup_inputs(seed: int = 0) -> dict:
    streams_of = jax.random.split(jax.random.key(seed), 9)
    return {
        "fixed_point": draw_fixed_point(jax.random.fold_in(streams_of[8], 71), 0),
        "upstream": draw_upstream(jax.random.fold_in(streams_of[8], 71), 0),
        "norm_gain": draw_norm_gain(jax.random.fold_in(streams_of[8], 71), 0),
        "query_weight": draw_query_weight(jax.random.fold_in(streams_of[8], 71), 0),
        "keyval_weight": draw_keyval_weight(jax.random.fold_in(streams_of[8], 71), 0),
        "output_weight": gaussian(streams_of[5], (HEADS * HEAD_DIM, D), (4 * HEADS * HEAD_DIM) ** -0.5, 0.09375, ((0, 4),)),
        "log_norm": draw_log_norm(jax.random.fold_in(streams_of[8], 71), 0),
        "attention_out": draw_attention_out(jax.random.fold_in(streams_of[8], 71), 0),
    }


norm_eps = 1e-05
mix_eps = 1e-06

def window_mask(block_id):
    key_pos = jnp.arange((WIN_DEVS + 1) * TOK_DEV).astype(jnp.int32)[None, :]
    query_pos = jnp.arange(TOK_DEV).astype(jnp.int32)[:, None]
    lowest = (WIN_DEVS - block_id) * TOK_DEV
    return (key_pos > query_pos) & (key_pos <= query_pos + WIN_DEVS * TOK_DEV) & (key_pos >= lowest)

def reference(fixed_point, upstream, norm_gain, query_weight, keyval_weight, output_weight, log_norm, attention_out):
    group_size = HEADS // KV_HEADS
    block_total = TOKENS // TOK_DEV
    key_span = (WIN_DEVS + 1) * TOK_DEV
    score_scale = HEAD_DIM ** (-0.5)
    latent = fixed_point.astype(jnp.float32)
    inverse = lax.rsqrt(lax.optimization_barrier(jnp.mean(latent * latent, axis=1, keepdims=True)) + norm_eps)
    normed = latent * inverse
    hidden = (normed * norm_gain).astype(jnp.bfloat16)
    queries = jnp.dot(hidden, query_weight, preferred_element_type=jnp.float32).astype(jnp.bfloat16)
    keyval = jnp.dot(hidden, keyval_weight, preferred_element_type=jnp.float32).astype(jnp.bfloat16)
    padding = jnp.zeros((WIN_DEVS * TOK_DEV, KV_HEADS * 2 * HEAD_DIM), jnp.bfloat16)
    padded = jnp.concatenate([padding, keyval], axis=0)
    block_ids = jnp.arange(block_total).astype(jnp.int32)

    def apply_map(current):
        grad_out = jnp.dot(current.astype(jnp.bfloat16), output_weight.T, preferred_element_type=jnp.float32)
        grad_outb = grad_out.astype(jnp.bfloat16)
        row_terms = lax.optimization_barrier(jnp.sum((grad_out * attention_out.astype(jnp.float32)).reshape(TOKENS, HEADS, HEAD_DIM), axis=2))

        def one_block(block_id):
            first_row = block_id * TOK_DEV
            query_blk = lax.dynamic_slice_in_dim(queries, first_row, TOK_DEV, 0).astype(jnp.float32)
            query_blk = query_blk.reshape(TOK_DEV, KV_HEADS, group_size, HEAD_DIM)
            window = lax.dynamic_slice_in_dim(padded, first_row, key_span, 0).astype(jnp.float32)
            window = window.reshape(key_span, KV_HEADS, 2, HEAD_DIM)
            key_rows = window[:, :, 0]
            value_rows = window[:, :, 1]
            norms_blk = lax.dynamic_slice_in_dim(log_norm, first_row, TOK_DEV, 1).reshape(KV_HEADS, group_size, TOK_DEV)
            grad_blk = lax.dynamic_slice_in_dim(grad_outb, first_row, TOK_DEV, 0).astype(jnp.float32)
            grad_blk = grad_blk.reshape(TOK_DEV, KV_HEADS, group_size, HEAD_DIM)
            terms_blk = lax.dynamic_slice_in_dim(row_terms, first_row, TOK_DEV, 0).T.reshape(KV_HEADS, group_size, TOK_DEV)
            scores = jnp.einsum('rcge,pce->cgrp', query_blk, key_rows) * score_scale
            allowed = window_mask(block_id)
            weights_blk = jnp.where(allowed, jnp.exp(scores - norms_blk[..., None]), 0.0)
            weights_blk = lax.optimization_barrier(weights_blk.astype(jnp.bfloat16)).astype(jnp.float32)
            grad_prob = jnp.einsum('rcge,pce->cgrp', grad_blk, value_rows)
            grad_score = weights_blk * (grad_prob - terms_blk[..., None])
            grad_score = lax.optimization_barrier(grad_score.astype(jnp.bfloat16)).astype(jnp.float32)
            grad_query = jnp.einsum('cgrp,pce->rcge', grad_score, key_rows) * score_scale
            grad_query = grad_query.reshape(TOK_DEV, HEADS * HEAD_DIM).astype(jnp.bfloat16)
            grad_key = jnp.einsum('cgrp,rcge->pce', grad_score, query_blk) * score_scale
            grad_value = jnp.einsum('cgrp,rcge->pce', weights_blk, grad_blk)
            key_terms = jnp.stack([grad_key, grad_value], axis=2).reshape(key_span, KV_HEADS * 2 * HEAD_DIM)
            return (grad_query, key_terms)
        grad_query, key_terms = lax.map(one_block, block_ids)
        grad_query = grad_query.reshape(TOKENS, HEADS * HEAD_DIM)
        key_terms = key_terms.reshape(block_total, WIN_DEVS + 1, TOK_DEV, KV_HEADS * 2 * HEAD_DIM)
        collected = jnp.zeros((block_total + WIN_DEVS, TOK_DEV, KV_HEADS * 2 * HEAD_DIM), jnp.float32)
        for offset in range(WIN_DEVS + 1):
            collected = collected.at[offset:offset + block_total].add(key_terms[:, offset])
        grad_keyval = collected[WIN_DEVS:].reshape(TOKENS, KV_HEADS * 2 * HEAD_DIM).astype(jnp.bfloat16)
        grad_hidden = jnp.dot(grad_query, query_weight.T, preferred_element_type=jnp.float32)
        grad_hidden = grad_hidden + jnp.dot(grad_keyval, keyval_weight.T, preferred_element_type=jnp.float32)
        scaled = grad_hidden * norm_gain
        return inverse * (scaled - normed * lax.optimization_barrier(jnp.mean(scaled * normed, axis=1, keepdims=True)))
    cotangent = upstream.astype(jnp.float32)
    last_image = cotangent
    last_residual = cotangent
    current = cotangent
    for offset in range(ITERS):
        mapped = cotangent + apply_map(current)
        residual = mapped - current
        change = residual - last_residual
        mixing = jnp.mean(change * residual) / (jnp.mean(change * change) + mix_eps)
        current = mapped - mixing * (mapped - last_image)
        last_image = mapped
        last_residual = residual
    return current
```

```python
import functools

import jax
import jax.numpy as jnp
from jax import lax
from jax.experimental import pallas as pl
from jax.experimental.pallas import tpu as pltpu
from jax.sharding import PartitionSpec as P

WIN = 4
ITERS = 3
GROUP = 4
NORM_EPS = 1e-05
MIX_EPS = 1e-06
MESH = pl.DeviceIdType.MESH
BF = jnp.bfloat16
F32 = jnp.float32

NT = (((1,), (1,)), ((), ()))


def dot(a, b, dims=(((1,), (0,)), ((), ()))):
    return lax.dot_general(a, b, dims, preferred_element_type=F32)


def kernel(
    dims,
    entries,
    fp_in,
    up_in,
    gain_ref,
    wq_in,
    wkv_in,
    wo_in,
    ln_ref,
    ao_ref,
    out_ref,
    fp,
    wq,
    wo,
    wkv,
    xs,
    kvwin,
    kt_send,
    kt_recv,
    own_kt,
    hid,
    qpad,
    dopad,
    ktr,
    p_t,
    ds_t,
    ao_t,
    gq,
    normed,
    inv,
    img,
    img_prev,
    w_prev,
    res_prev,
    pq_own,
    pq_other,
    rs1_send,
    rs1_recv,
    rs2_send,
    rs2_recv,
    red_a_send,
    red_a,
    red_b_send,
    red_b,
    red_c_send,
    red_c,
    mix,
    in_sem,
    kv_ssem,
    kv_rsem,
    wkv_ssem,
    wkv_rsem,
    kt_ssem,
    kt_rsem,
    rs_ssem,
    rs_rsem,
    ag_ssem,
    ag_rsem,
    a_ssem,
    a_rsem,
    b_ssem,
    b_rsem,
    c_ssem,
    c_rsem,
):
    nx, nz, ny = dims
    blocks = nx * nz * ny
    rows, width = fp.shape
    part = rows // GROUP
    heads = ln_ref.shape[0]
    edge = qpad.shape[1] // 2
    s = lax.axis_index("seq")
    h = lax.axis_index("head")
    x = lax.rem(s, nx)
    zh = lax.rem(lax.div(s, nx), nz)
    y = lax.div(s, nx * nz)
    zl = lax.div(h, 2)
    c = lax.rem(h, 2)
    sibling = zl * 2 + (1 - c)
    across = (1 - zl) * 2 + c
    mine = pl.ds(pl.multiple_of(h * part, part), part)

    def z_peer(d):
        peer = lax.rem(zh * GROUP + h + d, nz * GROUP)
        return (y * nz + lax.div(peer, GROUP)) * nx + x, lax.rem(peer, GROUP)

    def x_peer(d):
        return (y * nz + zh) * nx + lax.rem(x + d, nx), h

    def y_peer(d):
        return (lax.rem(y + d, ny) * nz + zh) * nx + x, h

    loads = [
        pltpu.make_async_copy(fp_in, fp, in_sem.at[0]),
        pltpu.make_async_copy(wkv_in, wkv.at[h], in_sem.at[1]),
        pltpu.make_async_copy(wq_in, wq, in_sem.at[2]),
        pltpu.make_async_copy(up_in, xs.at[0], in_sem.at[3]),
        pltpu.make_async_copy(wo_in, wo, in_sem.at[4]),
    ]
    for load in loads:
        load.start()

    kvwin[0:WIN] = jnp.zeros((WIN, rows, 2 * edge), BF)
    kt_recv[...] = jnp.zeros(kt_recv.shape, BF)

    barrier = pltpu.get_barrier_semaphore()

    def greet(device):
        pl.semaphore_signal(barrier, inc=1, device_id=device, device_id_type=MESH)

    for o in range(1, WIN + 1):

        @pl.when(s >= o)
        def _(o=o):
            for q in range(GROUP):
                greet((s - o, q))

        @pl.when(s + o < blocks)
        def _(o=o):
            for q in range(GROUP):
                greet((s + o, q))

    for d in range(1, nz * GROUP):
        greet(z_peer(d))
    for d in range(1, nx):
        greet(x_peer(d))
    for d in range(1, ny):
        greet(y_peer(d))
    greeted = (
        GROUP * (jnp.minimum(s, WIN) + jnp.minimum(blocks - 1 - s, WIN))
        + nz * GROUP - 1 + nx - 1 + ny - 1
    )

    gain = gain_ref[...]
    loads[0].wait()
    latent = fp[...].astype(F32)
    inverse = lax.rsqrt(jnp.mean(latent * latent, axis=1, keepdims=True) + NORM_EPS)
    hid[...] = (latent * inverse * gain).astype(BF)
    own_latent = fp[mine, :].astype(F32)
    own_inverse = lax.rsqrt(jnp.mean(own_latent * own_latent, axis=1, keepdims=True) + NORM_EPS)
    inv[...] = jnp.broadcast_to(own_inverse, inv.shape)
    normed[...] = own_latent * own_inverse
    loads[1].wait()
    kvwin[WIN] = dot(hid[...], wkv[h]).astype(BF)

    pl.semaphore_wait(barrier, greeted)

    def kv_copy(o):
        return pltpu.make_async_remote_copy(
            src_ref=kvwin.at[WIN],
            dst_ref=kvwin.at[WIN - o],
            send_sem=kv_ssem.at[o - 1],
            recv_sem=kv_rsem.at[o - 1],
            device_id=(s + o, h),
            device_id_type=MESH,
        )

    for o in range(WIN, 0, -1):

        @pl.when(s + o < blocks)
        def _(o=o):
            kv_copy(o).start()

    def wkv_copy(slot, owner, target):
        return pltpu.make_async_remote_copy(
            src_ref=wkv.at[owner],
            dst_ref=wkv.at[owner],
            send_sem=wkv_ssem.at[slot],
            recv_sem=wkv_rsem.at[slot],
            device_id=(s, target),
            device_id_type=MESH,
        )

    wkv_copy(0, h, sibling).start()
    wkv_copy(1, h, across).start()

    loads[2].wait()
    queries = dot(hid[...], wq[...]).astype(BF)
    zero_half = jnp.zeros((rows, edge), BF)
    for i in range(heads):
        scaled_q = (queries[:, i * edge : (i + 1) * edge].astype(F32) * (edge ** -0.5)).astype(BF)
        qpad[i * rows : (i + 1) * rows, :] = jnp.concatenate([scaled_q, zero_half], axis=1)
    ao_t[...] = ao_ref[...].astype(F32).T
    log_row = jnp.concatenate([ln_ref[i : i + 1, :] for i in range(heads)], axis=1)
    dopad[0:edge, :] = jnp.zeros((edge, heads * rows), BF)
    loads[3].wait()
    base_own = xs[0, mine, :].astype(F32)
    img[...] = base_own
    img_prev[...] = base_own
    res_prev[...] = base_own
    w_prev[...] = jnp.zeros_like(w_prev)
    mix[...] = jnp.zeros_like(mix)
    loads[4].wait()

    key_pos = lax.broadcasted_iota(jnp.int32, (rows, heads * rows), 0)
    query_pos = lax.rem(lax.broadcasted_iota(jnp.int32, (rows, heads * rows), 1), rows)
    for j in range(WIN, -1, -1):
        if j < WIN:

            @pl.when(s >= WIN - j)
            def _(j=j):
                kv_copy(WIN - j).wait_recv()

        block = kvwin[j]
        scores = dot(block, qpad[...], NT)
        weights = jnp.exp(scores - log_row)
        if j == 0:
            weights = jnp.where(key_pos > query_pos, weights, 0.0)
        if j == WIN:
            weights = jnp.where(key_pos <= query_pos, weights, 0.0)
        else:
            weights = jnp.where(s >= WIN - j, weights, 0.0)
        p_t[j] = weights.astype(BF)
        ktr[:, j * rows : (j + 1) * rows] = block.astype(F32).T[0:edge, :].astype(BF)

    def kt_copy(k, o, q):
        return pltpu.make_async_remote_copy(
            src_ref=kt_send.at[k, o, pl.ds(q * part, part), :],
            dst_ref=kt_recv.at[k, o, h],
            send_sem=kt_ssem.at[k, o * GROUP + q],
            recv_sem=kt_rsem.at[k, o * GROUP + h],
            device_id=(s - o, q),
            device_id_type=MESH,
        )

    def kt_arrival(k, o, q):
        return pltpu.make_async_remote_copy(
            src_ref=kt_send.at[k, o, pl.ds(0, part), :],
            dst_ref=kt_recv.at[k, o, q],
            send_sem=kt_ssem.at[k, o * GROUP + q],
            recv_sem=kt_rsem.at[k, o * GROUP + q],
            device_id=(s, q),
            device_id_type=MESH,
        )

    def rs1_copy(k):
        return pltpu.make_async_remote_copy(
            src_ref=rs1_send.at[k],
            dst_ref=rs1_recv.at[k],
            send_sem=rs_ssem.at[k, 0],
            recv_sem=rs_rsem.at[k, 0],
            device_id=(s, sibling),
            device_id_type=MESH,
        )

    def rs2_copy(k):
        return pltpu.make_async_remote_copy(
            src_ref=rs2_send.at[k],
            dst_ref=rs2_recv.at[k],
            send_sem=rs_ssem.at[k, 1],
            recv_sem=rs_rsem.at[k, 1],
            device_id=(s, across),
            device_id_type=MESH,
        )

    def ag_copy(k, slot, owner, target):
        span = pl.ds(pl.multiple_of(owner * part, part), part)
        return pltpu.make_async_remote_copy(
            src_ref=xs.at[k, span, :],
            dst_ref=xs.at[k, span, :],
            send_sem=ag_ssem.at[k - 1, slot],
            recv_sem=ag_rsem.at[k - 1, slot],
            device_id=(s, target),
            device_id_type=MESH,
        )

    def gathered(k):
        ag_copy(k, 1, across, across).wait_recv()
        ag_copy(k, 2, across, sibling).start()
        ag_copy(k, 0, sibling, sibling).wait_recv()
        ag_copy(k, 2, sibling, sibling).wait_recv()

    def red_copy(k, send, recv, ssem, rsem, d, me, peer):
        return pltpu.make_async_remote_copy(
            src_ref=send.at[k],
            dst_ref=recv.at[k, me],
            send_sem=ssem.at[k, d],
            recv_sem=rsem.at[k, d],
            device_id=peer,
            device_id_type=MESH,
        )

    stages = (
        (red_a_send, red_a, a_ssem, a_rsem, nz * GROUP, zh * GROUP + h, z_peer),
        (red_b_send, red_b, b_ssem, b_rsem, nx, x, x_peer),
        (red_c_send, red_c, c_ssem, c_rsem, ny, y, y_peer),
    )

    def red_start(k, stage, value):
        send, recv, ssem, rsem, count, me, peer = stages[stage]
        send[k] = value
        recv[k, me] = value
        for d in range(1, count):
            red_copy(k, send, recv, ssem, rsem, d, me, peer(d)).start()

    def red_finish(k, stage):
        send, recv, ssem, rsem, count, me, peer = stages[stage]
        for d in range(1, count):
            red_copy(k, send, recv, ssem, rsem, d, me, peer(d)).wait_recv()
        total = recv[k, 0]
        for i in range(1, count):
            total = total + recv[k, i]
        return total

    def set_mix(total):
        cross = jnp.sum(total[0:1, :], axis=1, keepdims=True)
        square = jnp.sum(total[1:2, :], axis=1, keepdims=True)
        mixing = cross / entries / (square / entries + MIX_EPS)
        mix[...] = jnp.broadcast_to(mixing, mix.shape)

    def step(k, carry):
        @pl.when(k > 0)
        def _():
            gathered(k)

        grad_out = dot(wo[...], xs[k], NT)
        terms = []
        for i in range(heads):
            piece = grad_out[i * edge : (i + 1) * edge, :]
            terms.append(
                jnp.sum(piece * ao_t[i * edge : (i + 1) * edge, :], axis=0, keepdims=True)
            )
            dopad[edge : 2 * edge, i * rows : (i + 1) * rows] = piece.astype(BF)
        row_terms = jnp.concatenate(terms, axis=1)

        @pl.when(k > 0)
        def _():
            red_start(k - 1, 1, red_finish(k - 1, 0))

        for j in range(WIN + 1):
            o = WIN - j
            probs = p_t[j]
            grad_prob = dot(kvwin[j], dopad[...])
            grad_score = (probs.astype(F32) * (grad_prob - row_terms)).astype(BF)
            ds_t[j * rows : (j + 1) * rows, :] = grad_score
            key_terms = dot(grad_score, qpad[...]) + dot(probs, dopad[...], NT)
            kt_send[k, o] = key_terms.astype(BF)
            if o > 0:

                @pl.when(s >= o)
                def _(o=o):
                    for q in range(GROUP):
                        kt_copy(k, o, q).start()

            else:
                own_kt[...] = key_terms
                for q in range(GROUP):

                    @pl.when(h != q)
                    def _(q=q):
                        kt_copy(k, 0, q).start()

        grad_q = dot(ktr[...], ds_t[...]) * (edge ** -0.5)
        gq[...] = (
            jnp.concatenate([grad_q[:, i * rows : (i + 1) * rows] for i in range(heads)], axis=0)
            .T.astype(BF)
        )

        def quarter(q):
            return gq[pl.ds(pl.multiple_of(q * part, part), part), :]

        theirs = jnp.concatenate([quarter(1 - c), quarter(3 - c)], axis=0)
        rs1_send[k] = dot(theirs, wq[...], NT).astype(BF).reshape(2, part, width)
        rs1_copy(k).start()
        ours = dot(jnp.concatenate([quarter(h), quarter(across)], axis=0), wq[...], NT)
        pq_own[...] = ours[:part]
        rs1_copy(k).wait_recv()
        rs2_send[k] = (ours[part:] + rs1_recv[k, 1 - zl].astype(F32)).astype(BF)
        rs2_copy(k).start()

        @pl.when(k > 0)
        def _():
            red_start(k - 1, 2, red_finish(k - 1, 1))

        @pl.when(k == 0)
        def _():
            wkv_copy(1, across, across).wait_recv()
            wkv_copy(2, across, sibling).start()

        for o in range(WIN + 1):
            for q in range(GROUP):
                if o > 0:

                    @pl.when(s + o < blocks)
                    def _(o=o, q=q):
                        kt_arrival(k, o, q).wait_recv()

                else:

                    @pl.when(h != q)
                    def _(q=q):
                        kt_arrival(k, 0, q).wait_recv()

        own_terms = own_kt[mine, :]
        collected = []
        for q in range(GROUP):
            total = jnp.where(h == q, own_terms, kt_recv[k, 0, q].astype(F32))
            for o in range(1, WIN + 1):
                total = total + kt_recv[k, o, q].astype(F32)
            collected.append(total.astype(BF))

        @pl.when(k == 0)
        def _():
            wkv_copy(0, sibling, sibling).wait_recv()
            wkv_copy(2, sibling, sibling).wait_recv()

        @pl.when(k > 0)
        def _():
            set_mix(red_finish(k - 1, 2))

        hidden_grad = pq_own[...] + rs1_recv[k, zl].astype(F32)
        for q in range(GROUP):
            hidden_grad = hidden_grad + dot(collected[q], wkv[q], NT)
        rs2_copy(k).wait_recv()
        hidden_grad = hidden_grad + rs2_recv[k].astype(F32)
        scaled = hidden_grad * gain_ref[...]
        own_normed = normed[...]
        mapped = inv[:, 0:1] * (
            scaled - own_normed * jnp.mean(scaled * own_normed, axis=1, keepdims=True)
        )
        mixing = mix[0:1, 0:1]
        base = xs[0, mine, :].astype(F32)
        last = img[...]
        current = last - mixing * (last - img_prev[...])
        image = base + (mapped - mixing * (mapped - w_prev[...]))
        xs[k + 1, mine, :] = image.astype(BF)
        ag_copy(k + 1, 1, h, across).start()
        ag_copy(k + 1, 0, h, sibling).start()
        residual = image - current
        change = residual - res_prev[...]

        def lanes(value):
            value = jnp.sum(value, axis=0, keepdims=True)
            total = value[:, 0:128]
            for i in range(1, width // 128):
                total = total + value[:, i * 128 : (i + 1) * 128]
            return total

        sums = jnp.concatenate(
            [lanes(change * residual), lanes(change * change), jnp.zeros((6, 128), F32)], axis=0
        )
        red_start(k, 0, sums)
        img_prev[...] = last
        img[...] = image
        w_prev[...] = mapped
        res_prev[...] = residual
        return carry

    lax.fori_loop(0, ITERS, step, 0)

    last = ITERS - 1
    red_start(last, 1, red_finish(last, 0))
    gathered(ITERS)
    red_start(last, 2, red_finish(last, 1))
    set_mix(red_finish(last, 2))
    final = xs[ITERS].astype(F32)
    out_ref[...] = final - mix[0:1, 0:1] * (final - xs[ITERS - 1].astype(F32))

    for o in range(1, WIN + 1):

        @pl.when(s + o < blocks)
        def _(o=o):
            kv_copy(o).wait_send()

    wkv_copy(0, h, sibling).wait_send()
    wkv_copy(1, h, across).wait_send()
    wkv_copy(2, across, sibling).wait_send()

    def drain(k, carry):
        for o in range(WIN + 1):
            for q in range(GROUP):
                if o > 0:

                    @pl.when(s >= o)
                    def _(o=o, q=q):
                        kt_copy(k, o, q).wait_send()

                else:

                    @pl.when(h != q)
                    def _(q=q):
                        kt_copy(k, 0, q).wait_send()

        rs1_copy(k).wait_send()
        rs2_copy(k).wait_send()
        ag_copy(k + 1, 0, h, sibling).wait_send()
        ag_copy(k + 1, 1, h, across).wait_send()
        ag_copy(k + 1, 2, across, sibling).wait_send()
        for send, recv, ssem, rsem, count, me, peer in stages:
            for d in range(1, count):
                red_copy(k, send, recv, ssem, rsem, d, me, peer(d)).wait_send()
        return carry

    lax.fori_loop(0, ITERS, drain, 0)


def shards(dims, fixed_point, upstream, norm_gain, query_weight, keyval_weight, output_weight, log_norm, attention_out):
    rows, width = fixed_point.shape
    nx, nz, ny = dims
    heads = log_norm.shape[0]
    cols = query_weight.shape[1]
    kv_cols = keyval_weight.shape[1]
    part = rows // GROUP
    keys = (WIN + 1) * rows
    entries = rows * nx * nz * ny * width
    hbm = pl.BlockSpec(memory_space=pl.ANY)
    vmem = pl.BlockSpec(memory_space=pltpu.VMEM)
    dma = pltpu.SemaphoreType.DMA
    state = pltpu.VMEM((part, width), F32)
    scratch = [
        pltpu.VMEM((rows, width), BF),
        pltpu.VMEM((width, cols), BF),
        pltpu.VMEM((cols, width), BF),
        pltpu.VMEM((GROUP, width, kv_cols), BF),
        pltpu.VMEM((ITERS + 1, rows, width), BF),
        pltpu.VMEM((WIN + 1, rows, kv_cols), BF),
        pltpu.VMEM((ITERS, WIN + 1, rows, kv_cols), BF),
        pltpu.VMEM((ITERS, WIN + 1, GROUP, part, kv_cols), BF),
        pltpu.VMEM((rows, kv_cols), F32),
        pltpu.VMEM((rows, width), BF),
        pltpu.VMEM((heads * rows, kv_cols), BF),
        pltpu.VMEM((kv_cols, heads * rows), BF),
        pltpu.VMEM((kv_cols // 2, keys), BF),
        pltpu.VMEM((WIN + 1, rows, heads * rows), BF),
        pltpu.VMEM((keys, heads * rows), BF),
        pltpu.VMEM((cols, rows), F32),
        pltpu.VMEM((rows, cols), BF),
        state,
        pltpu.VMEM((part, 128), F32),
        state,
        state,
        state,
        state,
        state,
        state,
        pltpu.VMEM((ITERS, 2, part, width), BF),
        pltpu.VMEM((ITERS, 2, part, width), BF),
        pltpu.VMEM((ITERS, part, width), BF),
        pltpu.VMEM((ITERS, part, width), BF),
        pltpu.VMEM((ITERS, 8, 128), F32),
        pltpu.VMEM((ITERS, nz * GROUP, 8, 128), F32),
        pltpu.VMEM((ITERS, 8, 128), F32),
        pltpu.VMEM((ITERS, nx, 8, 128), F32),
        pltpu.VMEM((ITERS, 8, 128), F32),
        pltpu.VMEM((ITERS, ny, 8, 128), F32),
        pltpu.VMEM((8, 128), F32),
        dma((5,)),
        dma((WIN,)),
        dma((WIN,)),
        dma((3,)),
        dma((3,)),
        dma((ITERS, (WIN + 1) * GROUP)),
        dma((ITERS, (WIN + 1) * GROUP)),
        dma((ITERS, 2)),
        dma((ITERS, 2)),
        dma((ITERS, 3)),
        dma((ITERS, 3)),
        dma((ITERS, nz * GROUP)),
        dma((ITERS, nz * GROUP)),
        dma((ITERS, nx)),
        dma((ITERS, nx)),
        dma((ITERS, ny)),
        dma((ITERS, ny)),
    ]
    return pl.pallas_call(
        functools.partial(kernel, dims, float(entries)),
        out_shape=jax.ShapeDtypeStruct((rows, width), F32),
        in_specs=[hbm, hbm, vmem, hbm, hbm, hbm, vmem, vmem],
        out_specs=vmem,
        scratch_shapes=scratch,
        compiler_params=pltpu.CompilerParams(
            collective_id=0, has_side_effects=True, vmem_limit_bytes=58 << 20
        ),
        name="adjoint",
    )(
        fixed_point,
        upstream,
        norm_gain.reshape(1, width),
        query_weight,
        keyval_weight,
        output_weight,
        log_norm,
        attention_out,
    )


def solution(mesh, dims=(4, 4, 8)):
    in_specs = (
        P("seq", None),
        P("seq", None),
        P(),
        P(None, "head"),
        P(None, "head"),
        P("head", None),
        P("head", "seq"),
        P("seq", "head"),
    )
    return jax.shard_map(
        functools.partial(shards, dims),
        mesh=mesh,
        in_specs=in_specs,
        out_specs=P("seq", None),
        check_vma=False,
    )
```

```python
import functools

import jax
import jax.numpy as jnp
from jax import lax
from jax.experimental import pallas as pl
from jax.experimental.pallas import tpu as pltpu
from jax.sharding import PartitionSpec as P

WIN = 4
ITERS = 3
GROUP = 4
NORM_EPS = 1e-05
MIX_EPS = 1e-06
MESH = pl.DeviceIdType.MESH
BF = jnp.bfloat16
F32 = jnp.float32

NT = (((1,), (1,)), ((), ()))


def dot(a, b, dims=(((1,), (0,)), ((), ()))):
    return lax.dot_general(a, b, dims, preferred_element_type=F32)


def kernel(
    dims,
    entries,
    fp_in,
    up_in,
    gain_ref,
    wq_in,
    wkv_in,
    wo_in,
    ln_ref,
    ao_ref,
    last_out,
    prev_out,
    mix_out,
    fp,
    wq,
    wo,
    wkv,
    xs,
    kvwin,
    kt_send,
    kt_recv,
    own_kt,
    hid,
    qpad,
    dopad,
    ktr,
    p_t,
    ds_t,
    ao_t,
    gq,
    normed,
    inv,
    img,
    img_prev,
    w_prev,
    res_prev,
    pq_own,
    rs_send,
    rs_recv,
    red_a_send,
    red_a,
    red_b_send,
    red_b,
    red_c_send,
    red_c,
    mix,
    in_sem,
    kv_ssem,
    kv_rsem,
    wkv_ssem,
    wkv_rsem,
    kt_ssem,
    kt_rsem,
    rs_ssem,
    rs_rsem,
    ag_ssem,
    ag_rsem,
    a_ssem,
    a_rsem,
    b_ssem,
    b_rsem,
    c_ssem,
    c_rsem,
):
    nx, nz, ny = dims
    blocks = nx * nz * ny
    rows, width = fp.shape
    part = rows // GROUP
    heads = ln_ref.shape[0]
    edge = qpad.shape[1] // 2
    s = lax.axis_index("seq")
    h = lax.axis_index("head")
    x = lax.rem(s, nx)
    zh = lax.rem(lax.div(s, nx), nz)
    y = lax.div(s, nx * nz)
    zl = lax.div(h, 2)
    c = lax.rem(h, 2)
    sibling = zl * 2 + (1 - c)
    across = (1 - zl) * 2 + c
    mine = pl.ds(pl.multiple_of(h * part, part), part)

    def z_peer(d):
        peer = lax.rem(zh * GROUP + h + d, nz * GROUP)
        return (y * nz + lax.div(peer, GROUP)) * nx + x, lax.rem(peer, GROUP)

    def x_peer(d):
        return (y * nz + zh) * nx + lax.rem(x + d, nx), h

    def y_peer(d):
        return (lax.rem(y + d, ny) * nz + zh) * nx + x, h

    loads = [
        pltpu.make_async_copy(fp_in, fp, in_sem.at[0]),
        pltpu.make_async_copy(wkv_in, wkv.at[h], in_sem.at[1]),
        pltpu.make_async_copy(wq_in, wq.at[c], in_sem.at[2]),
        pltpu.make_async_copy(up_in, xs.at[0], in_sem.at[3]),
        pltpu.make_async_copy(wo_in, wo, in_sem.at[4]),
    ]
    for load in loads:
        load.start()

    kvwin[0:WIN] = jnp.zeros((WIN, rows, 2 * edge), BF)
    kt_recv[...] = jnp.zeros(kt_recv.shape, BF)

    barrier = pltpu.get_barrier_semaphore()

    def greet(device):
        pl.semaphore_signal(barrier, inc=1, device_id=device, device_id_type=MESH)

    for o in range(1, WIN + 1):

        @pl.when(s >= o)
        def _(o=o):
            greet((s - o, h))

        @pl.when(s + o < blocks)
        def _(o=o):
            for q in range(GROUP):
                greet((s + o, q))

    for d in range(1, nz * GROUP):
        greet(z_peer(d))
    for d in range(1, nx):
        greet(x_peer(d))
    for d in range(1, ny):
        greet(y_peer(d))
    greeted = (
        GROUP * jnp.minimum(s, WIN) + jnp.minimum(blocks - 1 - s, WIN)
        + nz * GROUP - 1 + nx - 1 + ny - 1
    )

    gain = gain_ref[...]
    loads[0].wait()
    latent = fp[...].astype(F32)
    inverse = lax.rsqrt(jnp.mean(latent * latent, axis=1, keepdims=True) + NORM_EPS)
    hid[...] = (latent * inverse * gain).astype(BF)
    own_latent = fp[mine, :].astype(F32)
    own_inverse = lax.rsqrt(jnp.mean(own_latent * own_latent, axis=1, keepdims=True) + NORM_EPS)
    inv[...] = jnp.broadcast_to(own_inverse, inv.shape)
    normed[...] = own_latent * own_inverse
    loads[1].wait()
    kvwin[WIN] = dot(hid[...], wkv[h]).astype(BF)

    pl.semaphore_wait(barrier, greeted)

    def kv_copy(o):
        return pltpu.make_async_remote_copy(
            src_ref=kvwin.at[WIN],
            dst_ref=kvwin.at[WIN - o],
            send_sem=kv_ssem.at[o - 1],
            recv_sem=kv_rsem.at[o - 1],
            device_id=(s + o, h),
            device_id_type=MESH,
        )

    for o in range(WIN, 0, -1):

        @pl.when(s + o < blocks)
        def _(o=o):
            kv_copy(o).start()

    def wkv_copy(slot, owner, target):
        return pltpu.make_async_remote_copy(
            src_ref=wkv.at[owner],
            dst_ref=wkv.at[owner],
            send_sem=wkv_ssem.at[slot],
            recv_sem=wkv_rsem.at[slot],
            device_id=(s, target),
            device_id_type=MESH,
        )

    wkv_copy(0, h, sibling).start()
    wkv_copy(1, h, across).start()

    loads[2].wait()

    def wq_copy():
        return pltpu.make_async_remote_copy(
            src_ref=wq.at[c],
            dst_ref=wq.at[c],
            send_sem=wkv_ssem.at[3],
            recv_sem=wkv_rsem.at[3],
            device_id=(s, sibling),
            device_id_type=MESH,
        )

    wq_copy().start()
    queries = dot(hid[...], wq[c]).astype(BF)
    zero_half = jnp.zeros((rows, edge), BF)
    for i in range(heads):
        scaled_q = (queries[:, i * edge : (i + 1) * edge].astype(F32) * (edge ** -0.5)).astype(BF)
        qpad[i * rows : (i + 1) * rows, :] = jnp.concatenate([scaled_q, zero_half], axis=1)
    ao_t[...] = ao_ref[...].astype(F32).T
    log_row = jnp.concatenate([ln_ref[i : i + 1, :] for i in range(heads)], axis=1)
    dopad[0:edge, :] = jnp.zeros((edge, heads * rows), BF)
    loads[3].wait()
    base_own = xs[0, mine, :].astype(F32)
    img[...] = base_own
    img_prev[...] = base_own
    res_prev[...] = base_own
    w_prev[...] = jnp.zeros_like(w_prev)
    mix[...] = jnp.zeros_like(mix)
    loads[4].wait()

    def kt_copy(k, o, q):
        return pltpu.make_async_remote_copy(
            src_ref=kt_send.at[k, o, pl.ds(q * part, part), :],
            dst_ref=kt_recv.at[k, o, h],
            send_sem=kt_ssem.at[k, o * GROUP + q],
            recv_sem=kt_rsem.at[k, o * GROUP + h],
            device_id=(s - o, q),
            device_id_type=MESH,
        )

    def kt_arrival(k, o, q):
        return pltpu.make_async_remote_copy(
            src_ref=kt_send.at[k, o, pl.ds(0, part), :],
            dst_ref=kt_recv.at[k, o, q],
            send_sem=kt_ssem.at[k, o * GROUP + q],
            recv_sem=kt_rsem.at[k, o * GROUP + q],
            device_id=(s, q),
            device_id_type=MESH,
        )

    def gq_copy(k):
        return pltpu.make_async_remote_copy(
            src_ref=gq.at[k, c],
            dst_ref=gq.at[k, c],
            send_sem=rs_ssem.at[k, 0],
            recv_sem=rs_rsem.at[k, 0],
            device_id=(s, sibling),
            device_id_type=MESH,
        )

    def rs_copy(k, n):
        return pltpu.make_async_remote_copy(
            src_ref=rs_send.at[k, n],
            dst_ref=rs_recv.at[k, n],
            send_sem=rs_ssem.at[k, 1 + n],
            recv_sem=rs_rsem.at[k, 1 + n],
            device_id=(s, across),
            device_id_type=MESH,
        )

    def ag_copy(k, slot, owner, target):
        span = pl.ds(pl.multiple_of(owner * part, part), part)
        return pltpu.make_async_remote_copy(
            src_ref=xs.at[k, span, :],
            dst_ref=xs.at[k, span, :],
            send_sem=ag_ssem.at[k - 1, slot],
            recv_sem=ag_rsem.at[k - 1, slot],
            device_id=(s, target),
            device_id_type=MESH,
        )

    def gathered(k):
        ag_copy(k, 1, across, across).wait_recv()
        ag_copy(k, 2, across, sibling).start()
        ag_copy(k, 0, sibling, sibling).wait_recv()
        ag_copy(k, 2, sibling, sibling).wait_recv()

    def red_copy(k, send, recv, ssem, rsem, d, me, peer):
        return pltpu.make_async_remote_copy(
            src_ref=send.at[k],
            dst_ref=recv.at[k, me],
            send_sem=ssem.at[k, d],
            recv_sem=rsem.at[k, d],
            device_id=peer,
            device_id_type=MESH,
        )

    stages = (
        (red_a_send, red_a, a_ssem, a_rsem, nz * GROUP, zh * GROUP + h, z_peer),
        (red_b_send, red_b, b_ssem, b_rsem, nx, x, x_peer),
        (red_c_send, red_c, c_ssem, c_rsem, ny, y, y_peer),
    )

    def red_start(k, stage, value):
        send, recv, ssem, rsem, count, me, peer = stages[stage]
        send[k] = value
        recv[k, me] = value
        for d in range(1, count):
            red_copy(k, send, recv, ssem, rsem, d, me, peer(d)).start()

    def red_finish(k, stage):
        send, recv, ssem, rsem, count, me, peer = stages[stage]
        for d in range(1, count):
            red_copy(k, send, recv, ssem, rsem, d, me, peer(d)).wait_recv()
        total = recv[k, 0]
        for i in range(1, count):
            total = total + recv[k, i]
        return total

    def set_mix(total):
        first = lax.broadcasted_iota(jnp.int32, total.shape, 1) < 64
        cross = jnp.sum(jnp.where(first, total, 0.0), axis=1, keepdims=True)
        square = jnp.sum(jnp.where(first, 0.0, total), axis=1, keepdims=True)
        mixing = cross / entries / (square / entries + MIX_EPS)
        mix[...] = jnp.broadcast_to(mixing, mix.shape)

    key_pos = lax.broadcasted_iota(jnp.int32, (rows, heads * rows), 0)
    query_pos = lax.rem(lax.broadcasted_iota(jnp.int32, (rows, heads * rows), 1), rows)

    def probabilities(j):
        block = kvwin[j]
        weights = jnp.exp(dot(block, qpad[...], NT) - log_row)
        if j == 0:
            weights = jnp.where(key_pos > query_pos, weights, 0.0)
        if j == WIN:
            weights = jnp.where(key_pos <= query_pos, weights, 0.0)
        else:
            weights = jnp.where(s >= WIN - j, weights, 0.0)
        p_t[j] = weights.astype(BF)
        ktr[:, j * rows : (j + 1) * rows] = block.astype(F32).T[0:edge, :].astype(BF)

    def head_cotangents(k):
        grad_out = dot(wo[...], xs[k], NT)
        terms = []
        for i in range(heads):
            piece = grad_out[i * edge : (i + 1) * edge, :]
            terms.append(
                jnp.sum(piece * ao_t[i * edge : (i + 1) * edge, :], axis=0, keepdims=True)
            )
            dopad[edge : 2 * edge, i * rows : (i + 1) * rows] = piece.astype(BF)
        return jnp.concatenate(terms, axis=1)

    def block_terms(k, j, row_terms):
        o = WIN - j
        probs = p_t[j]
        grad_prob = dot(kvwin[j], dopad[...])
        grad_score = (probs.astype(F32) * (grad_prob - row_terms)).astype(BF)
        ds_t[j * rows : (j + 1) * rows, :] = grad_score
        key_terms = dot(grad_score, qpad[...]) + dot(probs, dopad[...], NT)
        kt_send[k, o] = key_terms.astype(BF)
        if o > 0:

            @pl.when(s >= o)
            def _():
                for q in range(GROUP):
                    kt_copy(k, o, q).start()

        else:
            own_kt[...] = key_terms
            for q in range(GROUP):

                @pl.when(h != q)
                def _(q=q):
                    kt_copy(k, 0, q).start()

    def finish(k, first):
        grad_q = dot(ktr[...], ds_t[...]) * (edge ** -0.5)
        gq[k, c] = (
            jnp.concatenate([grad_q[:, i * rows : (i + 1) * rows] for i in range(heads)], axis=0)
            .T.astype(BF)
        )
        gq_copy(k).start()
        if first:
            wkv_copy(1, across, across).wait_recv()
            wkv_copy(2, across, sibling).start()
            wq_copy().wait_recv()
        else:
            red_start(k - 1, 2, red_finish(k - 1, 1))
        gq_copy(k).wait_recv()
        theirs = pl.ds(pl.multiple_of(across * part, part), part)
        for n in range(2):
            half = slice(n * (width // 2), (n + 1) * (width // 2))
            total = jnp.zeros((2 * part, width // 2), F32)
            for i in range(2):
                pair = jnp.concatenate([gq[k, i, theirs, :], gq[k, i, mine, :]], axis=0)
                total = total + dot(pair, wq[i, half, :], NT)
            rs_send[k, n] = total[:part].astype(BF)
            rs_copy(k, n).start()
            pq_own[:, half] = total[part:]

        for o in range(WIN + 1):
            for q in range(GROUP):
                if o > 0:

                    @pl.when(s + o < blocks)
                    def _(o=o, q=q):
                        kt_arrival(k, o, q).wait_recv()

                else:

                    @pl.when(h != q)
                    def _(q=q):
                        kt_arrival(k, 0, q).wait_recv()

        own_terms = own_kt[mine, :]
        collected = []
        for q in range(GROUP):
            total = jnp.where(h == q, own_terms, kt_recv[k, 0, q].astype(F32))
            for o in range(1, WIN + 1):
                total = total + kt_recv[k, o, q].astype(F32)
            collected.append(total.astype(BF))

        if first:
            wkv_copy(0, sibling, sibling).wait_recv()
            wkv_copy(2, sibling, sibling).wait_recv()
        else:
            set_mix(red_finish(k - 1, 2))

        hidden_grad = pq_own[...]
        for q in range(GROUP):
            hidden_grad = hidden_grad + dot(collected[q], wkv[q], NT)
        for n in range(2):
            rs_copy(k, n).wait_recv()
        hidden_grad = hidden_grad + jnp.concatenate(
            [rs_recv[k, 0], rs_recv[k, 1]], axis=1
        ).astype(F32)
        scaled = hidden_grad * gain_ref[...]
        own_normed = normed[...]
        mapped = inv[:, 0:1] * (
            scaled - own_normed * jnp.mean(scaled * own_normed, axis=1, keepdims=True)
        )
        mixing = mix[0:1, 0:1]
        base = xs[0, mine, :].astype(F32)
        last = img[...]
        current = last - mixing * (last - img_prev[...])
        image = base + (mapped - mixing * (mapped - w_prev[...]))
        xs[k + 1, mine, :] = image.astype(BF)
        ag_copy(k + 1, 1, h, across).start()
        ag_copy(k + 1, 0, h, sibling).start()
        residual = image - current
        change = residual - res_prev[...]

        def lanes(value):
            value = jnp.sum(value, axis=0, keepdims=True)
            total = value[:, 0:128]
            for i in range(1, width // 128):
                total = total + value[:, i * 128 : (i + 1) * 128]
            return total

        crosses = lanes(change * residual)
        squares = lanes(change * change)
        first = lax.broadcasted_iota(jnp.int32, crosses.shape, 1) < 64
        sums = jnp.where(
            first, crosses + pltpu.roll(crosses, 64, 1), squares + pltpu.roll(squares, 64, 1)
        )
        red_start(k, 0, sums)
        img_prev[...] = last
        img[...] = image
        w_prev[...] = mapped
        res_prev[...] = residual

    row_terms = head_cotangents(0)
    for j in range(WIN, -1, -1):
        if j < WIN:

            @pl.when(s >= WIN - j)
            def _(j=j):
                kv_copy(WIN - j).wait_recv()

        probabilities(j)
        block_terms(0, j, row_terms)
    finish(0, True)

    def step(k, carry):
        gathered(k)
        row_terms = head_cotangents(k)
        red_start(k - 1, 1, red_finish(k - 1, 0))
        for j in range(WIN + 1):
            block_terms(k, j, row_terms)
        finish(k, False)
        return carry

    lax.fori_loop(1, ITERS, step, 0)


    last = ITERS - 1
    before = pltpu.make_async_copy(xs.at[last], prev_out, in_sem.at[5])
    before.start()
    red_start(last, 1, red_finish(last, 0))
    gathered(ITERS)
    after = pltpu.make_async_copy(xs.at[ITERS], last_out, in_sem.at[6])
    after.start()
    red_start(last, 2, red_finish(last, 1))
    set_mix(red_finish(last, 2))
    mix_out[...] = mix[0:1, 0:1]
    before.wait()
    after.wait()

    for o in range(1, WIN + 1):

        @pl.when(s + o < blocks)
        def _(o=o):
            kv_copy(o).wait_send()

    wkv_copy(0, h, sibling).wait_send()
    wkv_copy(1, h, across).wait_send()
    wkv_copy(2, across, sibling).wait_send()
    wq_copy().wait_send()

    def drain(k, carry):
        for o in range(WIN + 1):
            for q in range(GROUP):
                if o > 0:

                    @pl.when(s >= o)
                    def _(o=o, q=q):
                        kt_copy(k, o, q).wait_send()

                else:

                    @pl.when(h != q)
                    def _(q=q):
                        kt_copy(k, 0, q).wait_send()

        gq_copy(k).wait_send()
        rs_copy(k, 0).wait_send()
        rs_copy(k, 1).wait_send()
        ag_copy(k + 1, 0, h, sibling).wait_send()
        ag_copy(k + 1, 1, h, across).wait_send()
        ag_copy(k + 1, 2, across, sibling).wait_send()
        for send, recv, ssem, rsem, count, me, peer in stages:
            for d in range(1, count):
                red_copy(k, send, recv, ssem, rsem, d, me, peer(d)).wait_send()
        return carry

    lax.fori_loop(0, ITERS, drain, 0)


def shards(dims, fixed_point, upstream, norm_gain, query_weight, keyval_weight, output_weight, log_norm, attention_out):
    rows, width = fixed_point.shape
    nx, nz, ny = dims
    heads = log_norm.shape[0]
    cols = query_weight.shape[1]
    kv_cols = keyval_weight.shape[1]
    part = rows // GROUP
    keys = (WIN + 1) * rows
    entries = rows * nx * nz * ny * width
    hbm = pl.BlockSpec(memory_space=pl.ANY)
    vmem = pl.BlockSpec(memory_space=pltpu.VMEM)
    dma = pltpu.SemaphoreType.DMA
    state = pltpu.VMEM((part, width), F32)
    scratch = [
        pltpu.VMEM((rows, width), BF),
        pltpu.VMEM((2, width, cols), BF),
        pltpu.VMEM((cols, width), BF),
        pltpu.VMEM((GROUP, width, kv_cols), BF),
        pltpu.VMEM((ITERS + 1, rows, width), BF),
        pltpu.VMEM((WIN + 1, rows, kv_cols), BF),
        pltpu.VMEM((ITERS, WIN + 1, rows, kv_cols), BF),
        pltpu.VMEM((ITERS, WIN + 1, GROUP, part, kv_cols), BF),
        pltpu.VMEM((rows, kv_cols), F32),
        pltpu.VMEM((rows, width), BF),
        pltpu.VMEM((heads * rows, kv_cols), BF),
        pltpu.VMEM((kv_cols, heads * rows), BF),
        pltpu.VMEM((kv_cols // 2, keys), BF),
        pltpu.VMEM((WIN + 1, rows, heads * rows), BF),
        pltpu.VMEM((keys, heads * rows), BF),
        pltpu.VMEM((cols, rows), F32),
        pltpu.VMEM((ITERS, 2, rows, cols), BF),
        state,
        pltpu.VMEM((part, 128), F32),
        state,
        state,
        state,
        state,
        state,
        pltpu.VMEM((ITERS, 2, part, width // 2), BF),
        pltpu.VMEM((ITERS, 2, part, width // 2), BF),
        pltpu.VMEM((ITERS, 1, 128), F32),
        pltpu.VMEM((ITERS, nz * GROUP, 1, 128), F32),
        pltpu.VMEM((ITERS, 1, 128), F32),
        pltpu.VMEM((ITERS, nx, 1, 128), F32),
        pltpu.VMEM((ITERS, 1, 128), F32),
        pltpu.VMEM((ITERS, ny, 1, 128), F32),
        pltpu.VMEM((8, 128), F32),
        dma((7,)),
        dma((WIN,)),
        dma((WIN,)),
        dma((4,)),
        dma((4,)),
        dma((ITERS, (WIN + 1) * GROUP)),
        dma((ITERS, (WIN + 1) * GROUP)),
        dma((ITERS, 3)),
        dma((ITERS, 3)),
        dma((ITERS, 3)),
        dma((ITERS, 3)),
        dma((ITERS, nz * GROUP)),
        dma((ITERS, nz * GROUP)),
        dma((ITERS, nx)),
        dma((ITERS, nx)),
        dma((ITERS, ny)),
        dma((ITERS, ny)),
    ]
    last_image, previous, mixing = pl.pallas_call(
        functools.partial(kernel, dims, float(entries)),
        out_shape=(
            jax.ShapeDtypeStruct((rows, width), BF),
            jax.ShapeDtypeStruct((rows, width), BF),
            jax.ShapeDtypeStruct((1, 1), F32),
        ),
        in_specs=[hbm, hbm, vmem, hbm, hbm, hbm, vmem, vmem],
        out_specs=(hbm, hbm, vmem),
        scratch_shapes=scratch,
        compiler_params=pltpu.CompilerParams(
            collective_id=0, has_side_effects=True, vmem_limit_bytes=58 << 20
        ),
        name="adjoint",
    )(
        fixed_point,
        upstream,
        norm_gain.reshape(1, width),
        query_weight,
        keyval_weight,
        output_weight,
        log_norm,
        attention_out,
    )
    image = last_image.astype(F32)
    return image - mixing * (image - previous.astype(F32))


def solution(mesh, dims=(4, 4, 8)):
    in_specs = (
        P("seq", None),
        P("seq", None),
        P(),
        P(None, "head"),
        P(None, "head"),
        P("head", None),
        P("head", "seq"),
        P("seq", "head"),
    )
    return jax.shard_map(
        functools.partial(shards, dims),
        mesh=mesh,
        in_specs=in_specs,
        out_specs=P("seq", None),
        check_vma=False,
    )
```

```python
import functools

import jax
import jax.numpy as jnp
from jax import lax
from jax.experimental import pallas as pl
from jax.experimental.pallas import tpu as pltpu
from jax.sharding import PartitionSpec as P

WIN = 4
ITERS = 3
GROUP = 4
NORM_EPS = 1e-05
SCALE = 2.0**-12
RESCALE = SCALE**-2
PAIRS = [(i, j) for j in range(ITERS + 1) for i in range(j + 1)]
MIX_EPS = 1e-06
MESH = pl.DeviceIdType.MESH
BF = jnp.bfloat16
F32 = jnp.float32

NT = (((1,), (1,)), ((), ()))


def dot(a, b, dims=(((1,), (0,)), ((), ()))):
    return lax.dot_general(a, b, dims, preferred_element_type=F32)


def kernel(
    dims,
    entries,
    fp_in,
    up_in,
    gain_ref,
    wq_in,
    wkv_in,
    wo_in,
    ln_ref,
    ao_ref,
    xs_out,
    factor_1,
    factor_2,
    factor_3,
    fp,
    wq,
    wo,
    wkv,
    xs,
    kvwin,
    kt_send,
    kt_recv,
    own_kt,
    hid,
    qd,
    dopad,
    ktr,
    sp,
    ao_t,
    gq,
    normed,
    inv,
    krylov,
    pq_own,
    rs_send,
    rs_recv,
    red_a_send,
    red_a,
    red_b_send,
    red_b,
    red_c_send,
    red_c,
    gram,
    in_sem,
    kv_ssem,
    kv_rsem,
    wkv_ssem,
    wkv_rsem,
    kt_ssem,
    kt_rsem,
    rs_ssem,
    rs_rsem,
    ag_ssem,
    ag_rsem,
    red_ssem,
    red_rsem,
):
    factor_outs = (factor_1, factor_2, factor_3)
    nx, nz, ny = dims
    blocks = nx * nz * ny
    rows, width = fp.shape
    part = rows // GROUP
    heads = ln_ref.shape[0]
    edge = qd.shape[1] // 2
    span = heads * rows
    s = lax.axis_index("seq")
    h = lax.axis_index("head")
    x = lax.rem(s, nx)
    zh = lax.rem(lax.div(s, nx), nz)
    y = lax.div(s, nx * nz)
    zl = lax.div(h, 2)
    c = lax.rem(h, 2)
    sibling = zl * 2 + (1 - c)
    across = (1 - zl) * 2 + c
    mine = pl.ds(pl.multiple_of(h * part, part), part)

    def z_peer(d):
        peer = lax.rem(zh * GROUP + h + d, nz * GROUP)
        return (y * nz + lax.div(peer, GROUP)) * nx + x, lax.rem(peer, GROUP)

    def x_peer(d):
        return (y * nz + zh) * nx + lax.rem(x + d, nx), h

    def y_peer(d):
        return (lax.rem(y + d, ny) * nz + zh) * nx + x, h

    def wkv_of(owner):
        lanes = pl.ds(pl.multiple_of(lax.rem(owner, 2) * 2 * edge, 2 * edge), 2 * edge)
        return wkv.at[lax.div(owner, 2), :, lanes]

    loads = [
        pltpu.make_async_copy(fp_in, fp, in_sem.at[0]),
        pltpu.make_async_copy(wkv_in, wkv_of(h), in_sem.at[1]),
        pltpu.make_async_copy(wq_in, wq.at[c], in_sem.at[2]),
        pltpu.make_async_copy(up_in, xs.at[0], in_sem.at[3]),
        pltpu.make_async_copy(wo_in, wo, in_sem.at[4]),
    ]
    for load in loads:
        load.start()

    kvwin[0:WIN] = jnp.zeros((WIN, rows, 2 * edge), BF)
    kt_recv[...] = jnp.zeros(kt_recv.shape, BF)

    barrier = pltpu.get_barrier_semaphore()

    def greet(device):
        pl.semaphore_signal(barrier, inc=1, device_id=device, device_id_type=MESH)

    for o in range(1, WIN + 1):

        @pl.when(s >= o)
        def _(o=o):
            greet((s - o, h))

        @pl.when(s + o < blocks)
        def _(o=o):
            for q in range(GROUP):
                greet((s + o, q))

    for d in range(1, nz * GROUP):
        greet(z_peer(d))
    for d in range(1, nx):
        greet(x_peer(d))
    for d in range(1, ny):
        greet(y_peer(d))
    greeted = (
        GROUP * jnp.minimum(s, WIN) + jnp.minimum(blocks - 1 - s, WIN)
        + nz * GROUP - 1 + nx - 1 + ny - 1
    )

    gain = gain_ref[...]
    loads[0].wait()
    latent = fp[...].astype(F32)
    inverse = lax.rsqrt(jnp.mean(latent * latent, axis=1, keepdims=True) + NORM_EPS)
    hid[...] = (latent * inverse * gain).astype(BF)
    own_latent = fp[mine, :].astype(F32)
    own_inverse = lax.rsqrt(jnp.mean(own_latent * own_latent, axis=1, keepdims=True) + NORM_EPS)
    inv[...] = jnp.broadcast_to(own_inverse, inv.shape)
    normed[...] = own_latent * own_inverse
    loads[1].wait()
    kvwin[WIN] = dot(hid[...], wkv_of(h)[...]).astype(BF)

    pl.semaphore_wait(barrier, greeted)

    def kv_copy(o):
        return pltpu.make_async_remote_copy(
            src_ref=kvwin.at[WIN],
            dst_ref=kvwin.at[WIN - o],
            send_sem=kv_ssem.at[o - 1],
            recv_sem=kv_rsem.at[o - 1],
            device_id=(s + o, h),
            device_id_type=MESH,
        )

    for o in range(WIN, 0, -1):

        @pl.when(s + o < blocks)
        def _(o=o):
            kv_copy(o).start()

    def wkv_copy(slot, owner, target):
        return pltpu.make_async_remote_copy(
            src_ref=wkv_of(owner),
            dst_ref=wkv_of(owner),
            send_sem=wkv_ssem.at[slot],
            recv_sem=wkv_rsem.at[slot],
            device_id=(s, target),
            device_id_type=MESH,
        )

    wkv_copy(0, h, sibling).start()
    wkv_copy(1, h, across).start()

    loads[2].wait()

    def wq_copy():
        return pltpu.make_async_remote_copy(
            src_ref=wq.at[c],
            dst_ref=wq.at[c],
            send_sem=wkv_ssem.at[3],
            recv_sem=wkv_rsem.at[3],
            device_id=(s, sibling),
            device_id_type=MESH,
        )

    wq_copy().start()
    queries = dot(hid[...], wq[c]).astype(BF)
    zero_half = jnp.zeros((rows, edge), BF)
    for i in range(heads):
        scaled_q = (queries[:, i * edge : (i + 1) * edge].astype(F32) * (edge ** -0.5)).astype(BF)
        qd[i * rows : (i + 1) * rows, :] = jnp.concatenate([scaled_q, zero_half], axis=1)
    ao_t[...] = ao_ref[...].astype(F32).T
    log_row = jnp.concatenate([ln_ref[i : i + 1, :] for i in range(heads)], axis=1)
    dopad[0:edge, :] = jnp.zeros((edge, span), BF)
    qd[span:, 0:edge] = jnp.zeros((span, edge), BF)
    loads[3].wait()
    base_own = xs[0, mine, :].astype(F32)
    krylov[0] = base_own
    krylov[1:ITERS] = jnp.zeros((ITERS - 1,) + base_own.shape, F32)
    loads[4].wait()

    def kt_copy(k, o, q):
        return pltpu.make_async_remote_copy(
            src_ref=kt_send.at[k, WIN - o, pl.ds(q * part, part), :],
            dst_ref=kt_recv.at[k, o, h],
            send_sem=kt_ssem.at[k, o],
            recv_sem=kt_rsem.at[k, o],
            device_id=(s - o, q),
            device_id_type=MESH,
        )

    def kt_all(k, o):
        count = GROUP if o > 0 else GROUP - 1
        return pltpu.make_async_remote_copy(
            src_ref=kt_recv.at[k, o, pl.ds(0, count)],
            dst_ref=kt_recv.at[k, o, pl.ds(0, count)],
            send_sem=kt_ssem.at[k, o],
            recv_sem=kt_rsem.at[k, o],
            device_id=(s, sibling),
            device_id_type=MESH,
        )

    def gq_copy(k):
        return pltpu.make_async_remote_copy(
            src_ref=gq.at[k, c],
            dst_ref=gq.at[k, c],
            send_sem=rs_ssem.at[k, 0],
            recv_sem=rs_rsem.at[k, 0],
            device_id=(s, sibling),
            device_id_type=MESH,
        )

    def rs_copy(k, n):
        return pltpu.make_async_remote_copy(
            src_ref=rs_send.at[k, n],
            dst_ref=rs_recv.at[k, n],
            send_sem=rs_ssem.at[k, 1 + n],
            recv_sem=rs_rsem.at[k, 1 + n],
            device_id=(s, across),
            device_id_type=MESH,
        )

    def ag_copy(k, slot, owner, target):
        span = pl.ds(pl.multiple_of(owner * part, part), part)
        return pltpu.make_async_remote_copy(
            src_ref=xs.at[k, span, :],
            dst_ref=xs.at[k, span, :],
            send_sem=ag_ssem.at[k - 1, slot],
            recv_sem=ag_rsem.at[k - 1, slot],
            device_id=(s, target),
            device_id_type=MESH,
        )

    def gathered(k):
        ag_copy(k, 1, across, across).wait_recv()
        ag_copy(k, 2, across, sibling).start()
        ag_copy(k, 0, sibling, sibling).wait_recv()
        ag_copy(k, 2, sibling, sibling).wait_recv()

    stages = (
        (red_a_send, red_a, nz * GROUP, zh * GROUP + h, z_peer),
        (red_b_send, red_b, nx, x, x_peer),
        (red_c_send, red_c, ny, y, y_peer),
    )

    def red_all(stage):
        send, recv, count, me, peer = stages[stage]
        return pltpu.make_async_remote_copy(
            src_ref=recv.at[pl.ds(0, count - 1)],
            dst_ref=recv.at[pl.ds(0, count - 1)],
            send_sem=red_ssem.at[stage],
            recv_sem=red_rsem.at[stage],
            device_id=peer(1),
            device_id_type=MESH,
        )

    def red_start(stage, value):
        send, recv, count, me, peer = stages[stage]
        send[...] = value
        recv[me] = value
        for d in range(1, count):
            pltpu.make_async_remote_copy(
                src_ref=send,
                dst_ref=recv.at[me],
                send_sem=red_ssem.at[stage],
                recv_sem=red_rsem.at[stage],
                device_id=peer(d),
                device_id_type=MESH,
            ).start()

    def red_finish(stage):
        send, recv, count, me, peer = stages[stage]
        red_all(stage).wait_recv()
        total = recv[0]
        for i in range(1, count):
            total = total + recv[i]
        return total

    group_of_lane = lax.div(lax.broadcasted_iota(jnp.int32, (16, 128), 1), 8)
    row_of = lax.broadcasted_iota(jnp.int32, (16, 128), 0)

    def packed(sums):
        for shift in (64, 32, 16, 8):
            sums = sums + pltpu.roll(sums, shift, 1)
        return jnp.sum(jnp.where(group_of_lane == row_of, sums, 0.0), axis=0, keepdims=True)

    def coefficients(total):
        spread = jnp.where(group_of_lane == row_of, jnp.broadcast_to(total, (16, 128)), 0.0)
        column = jnp.sum(spread, axis=1, keepdims=True)
        index = {pair: i for i, pair in enumerate(PAIRS)}

        def inner(a, b):
            value = 0.0
            for i, left in enumerate(a):
                for j, right in enumerate(b):
                    if left is not None and right is not None:
                        at = index[min(i, j), max(i, j)]
                        value = value + left * right * column[at : at + 1, :]
            return value

        def combined(a, b, factor):
            out = []
            for left, right in zip(a, b):
                if right is None:
                    out.append(left)
                else:
                    out.append(factor * right if left is None else left + factor * right)
            return out

        one = jnp.ones((1, 1), F32)
        base = [one] + [None] * ITERS
        last_image, last_residual, current = base, base, base
        for _ in range(ITERS):
            image = combined(base, [None] + current[:ITERS], 1.0)
            residual = combined(image, current, -1.0)
            change = combined(residual, last_residual, -1.0)
            cross = inner(change, residual) * (RESCALE / entries)
            square = inner(change, change) * (RESCALE / entries)
            mixing = cross / (square + MIX_EPS)
            current = combined(image, combined(image, last_image, -1.0), -mixing)
            last_image, last_residual = image, residual
        return current

    key_pos = lax.broadcasted_iota(jnp.int32, (rows, span), 0)
    query_pos = lax.rem(lax.broadcasted_iota(jnp.int32, (rows, span), 1), rows)

    def probabilities(j):
        block = kvwin[j]
        weights = jnp.exp(dot(block, qd[0:span, :], NT) - log_row)
        if j == 0:
            weights = jnp.where(key_pos > query_pos, weights, 0.0)
        if j == WIN:
            weights = jnp.where(key_pos <= query_pos, weights, 0.0)
        else:
            weights = jnp.where(s >= WIN - j, weights, 0.0)
        sp[j * rows : (j + 1) * rows, span:] = weights.astype(BF)
        ktr[:, j * rows : (j + 1) * rows] = block.astype(F32).T[0:edge, :].astype(BF)

    def head_cotangents(k):
        grad_out = dot(wo[...], xs[k], NT)
        terms = []
        for i in range(heads):
            piece = grad_out[i * edge : (i + 1) * edge, :]
            terms.append(
                jnp.sum(piece * ao_t[i * edge : (i + 1) * edge, :], axis=0, keepdims=True)
            )
            dopad[edge : 2 * edge, i * rows : (i + 1) * rows] = piece.astype(BF)
            qd[span + i * rows : span + (i + 1) * rows, edge:] = piece.T.astype(BF)
        return jnp.concatenate(terms, axis=1)

    def block_terms(k, low, high, row_terms):
        count = high - low
        keys = slice(low * rows, high * rows)
        grad_prob = dot(kvwin[low:high].reshape(count * rows, 2 * edge), dopad[...])
        probs = sp[keys, span:]
        sp[keys, :span] = (probs.astype(F32) * (grad_prob - row_terms)).astype(BF)
        key_terms = dot(sp[keys, :], qd[...])
        kt_send[k, low:high] = key_terms.astype(BF).reshape(count, rows, 2 * edge)
        if high == WIN + 1:
            own_kt[...] = key_terms[(count - 1) * rows :]
        for j in range(low, high):
            o = WIN - j
            if o > 0:

                @pl.when(s >= o)
                def _(o=o):
                    for q in range(GROUP):
                        kt_copy(k, o, q).start()

            else:
                for q in range(GROUP):

                    @pl.when(h != q)
                    def _(q=q):
                        kt_copy(k, 0, q).start()

    def lanes(value):
        value = jnp.sum(value, axis=0, keepdims=True)
        total = value[:, 0:128]
        for i in range(1, width // 128):
            total = total + value[:, i * 128 : (i + 1) * 128]
        return total

    def add_inner(newest, count):
        right = krylov[newest] * SCALE
        row = lax.div(newest * (newest + 1), 2)
        for i in range(count):
            gram[pl.ds(row + i, 1), :] = lanes(krylov[i] * SCALE * right)

    def finish(k, first):
        grad_q = dot(ktr[...], sp[:, :span]) * (edge ** -0.5)
        gq[k, c] = (
            jnp.concatenate([grad_q[:, i * rows : (i + 1) * rows] for i in range(heads)], axis=0)
            .T.astype(BF)
        )
        gq_copy(k).start()
        add_inner(jnp.int32(k), ITERS)
        if first:
            wkv_copy(1, across, across).wait_recv()
            wkv_copy(2, across, sibling).start()
            wq_copy().wait_recv()
        gq_copy(k).wait_recv()
        theirs = pl.ds(pl.multiple_of(across * part, part), part)
        for n in range(2):
            half = slice(n * (width // 2), (n + 1) * (width // 2))
            total = jnp.zeros((2 * part, width // 2), F32)
            for i in range(2):
                pair = jnp.concatenate([gq[k, i, theirs, :], gq[k, i, mine, :]], axis=0)
                total = total + dot(pair, wq[i, half, :], NT)
            rs_send[k, n] = total[:part].astype(BF)
            rs_copy(k, n).start()
            pq_own[:, half] = total[part:]

        for o in range(1, WIN + 1):

            @pl.when(s + o < blocks)
            def _(o=o):
                kt_all(k, o).wait_recv()

        kt_all(k, 0).wait_recv()
        own_terms = own_kt[mine, :]
        collected = []
        for q in range(GROUP):
            total = jnp.where(h == q, own_terms, kt_recv[k, 0, q].astype(F32))
            for o in range(1, WIN + 1):
                total = total + kt_recv[k, o, q].astype(F32)
            collected.append(total.astype(BF))

        if first:
            wkv_copy(0, sibling, sibling).wait_recv()
            wkv_copy(2, sibling, sibling).wait_recv()

        hidden_grad = pq_own[...]
        for i in range(2):
            pair = jnp.concatenate(collected[2 * i : 2 * i + 2], axis=1)
            hidden_grad = hidden_grad + dot(pair, wkv[i], NT)
        for n in range(2):
            rs_copy(k, n).wait_recv()
        hidden_grad = hidden_grad + jnp.concatenate(
            [rs_recv[k, 0], rs_recv[k, 1]], axis=1
        ).astype(F32)
        scaled = hidden_grad * gain_ref[...]
        own_normed = normed[...]
        mapped = inv[:, 0:1] * (
            scaled - own_normed * jnp.mean(scaled * own_normed, axis=1, keepdims=True)
        )
        xs[k + 1, mine, :] = mapped.astype(BF)
        ag_copy(k + 1, 1, h, across).start()
        ag_copy(k + 1, 0, h, sibling).start()
        krylov[k + 1] = mapped

    row_terms = head_cotangents(0)
    for j in range(WIN, -1, -1):
        if j < WIN:

            @pl.when(s >= WIN - j)
            def _(j=j):
                kv_copy(WIN - j).wait_recv()

        probabilities(j)
        block_terms(0, j, j + 1, row_terms)
    gram[...] = jnp.zeros_like(gram)
    finish(0, True)

    def step(k, carry):
        gathered(k)
        block_terms(k, 0, WIN + 1, head_cotangents(k))
        finish(k, False)
        return carry

    lax.fori_loop(1, ITERS, step, 0)

    add_inner(jnp.int32(ITERS), ITERS + 1)
    red_start(0, packed(gram[...]))
    total = red_finish(0)
    red_start(1, total)
    gathered(ITERS)
    kept = pltpu.make_async_copy(xs.at[pl.ds(1, ITERS)], xs_out, in_sem.at[5])
    kept.start()
    total = red_finish(1)
    red_start(2, total)
    factors = coefficients(red_finish(2))
    for i in range(ITERS):
        factor_outs[i][...] = factors[i + 1]
    kept.wait()

    for o in range(1, WIN + 1):

        @pl.when(s + o < blocks)
        def _(o=o):
            kv_copy(o).wait_send()

    wkv_copy(0, h, sibling).wait_send()
    wkv_copy(1, h, across).wait_send()
    wkv_copy(2, across, sibling).wait_send()
    wq_copy().wait_send()

    for stage in range(3):
        red_all(stage).wait_send()

    def drain(k, carry):
        for o in range(1, WIN + 1):

            @pl.when(s >= o)
            def _(o=o):
                kt_all(k, o).wait_send()

        kt_all(k, 0).wait_send()
        gq_copy(k).wait_send()
        rs_copy(k, 0).wait_send()
        rs_copy(k, 1).wait_send()
        ag_copy(k + 1, 0, h, sibling).wait_send()
        ag_copy(k + 1, 1, h, across).wait_send()
        ag_copy(k + 1, 2, across, sibling).wait_send()
        return carry

    lax.fori_loop(0, ITERS, drain, 0)


def shards(dims, fixed_point, upstream, norm_gain, query_weight, keyval_weight, output_weight, log_norm, attention_out):
    rows, width = fixed_point.shape
    nx, nz, ny = dims
    heads = log_norm.shape[0]
    cols = query_weight.shape[1]
    kv_cols = keyval_weight.shape[1]
    part = rows // GROUP
    keys = (WIN + 1) * rows
    entries = rows * nx * nz * ny * width
    hbm = pl.BlockSpec(memory_space=pl.ANY)
    vmem = pl.BlockSpec(memory_space=pltpu.VMEM)
    dma = pltpu.SemaphoreType.DMA
    state = pltpu.VMEM((part, width), F32)
    scratch = [
        pltpu.VMEM((rows, width), BF),
        pltpu.VMEM((2, width, cols), BF),
        pltpu.VMEM((cols, width), BF),
        pltpu.VMEM((2, width, 2 * kv_cols), BF),
        pltpu.VMEM((ITERS + 1, rows, width), BF),
        pltpu.VMEM((WIN + 1, rows, kv_cols), BF),
        pltpu.VMEM((ITERS, WIN + 1, rows, kv_cols), BF),
        pltpu.VMEM((ITERS, WIN + 1, GROUP, part, kv_cols), BF),
        pltpu.VMEM((rows, kv_cols), F32),
        pltpu.VMEM((rows, width), BF),
        pltpu.VMEM((2 * heads * rows, kv_cols), BF),
        pltpu.VMEM((kv_cols, heads * rows), BF),
        pltpu.VMEM((kv_cols // 2, keys), BF),
        pltpu.VMEM((keys, 2 * heads * rows), BF),
        pltpu.VMEM((cols, rows), F32),
        pltpu.VMEM((ITERS, 2, rows, cols), BF),
        state,
        pltpu.VMEM((part, 128), F32),
        pltpu.VMEM((ITERS + 1, part, width), F32),
        state,
        pltpu.VMEM((ITERS, 2, part, width // 2), BF),
        pltpu.VMEM((ITERS, 2, part, width // 2), BF),
        pltpu.VMEM((1, 128), F32),
        pltpu.VMEM((nz * GROUP, 1, 128), F32),
        pltpu.VMEM((1, 128), F32),
        pltpu.VMEM((nx, 1, 128), F32),
        pltpu.VMEM((1, 128), F32),
        pltpu.VMEM((ny, 1, 128), F32),
        pltpu.VMEM((16, 128), F32),
        dma((7,)),
        dma((WIN,)),
        dma((WIN,)),
        dma((4,)),
        dma((4,)),
        dma((ITERS, WIN + 1)),
        dma((ITERS, WIN + 1)),
        dma((ITERS, 3)),
        dma((ITERS, 3)),
        dma((ITERS, 3)),
        dma((ITERS, 3)),
        dma((3,)),
        dma((3,)),
    ]
    images, *factors = pl.pallas_call(
        functools.partial(kernel, dims, float(entries)),
        out_shape=(
            pltpu.VMEM((ITERS, rows, width), BF),
        )
        + (jax.ShapeDtypeStruct((1, 1), F32),) * ITERS,
        in_specs=[hbm, hbm, vmem, hbm, hbm, hbm, vmem, vmem],
        out_specs=(vmem,) + (vmem,) * ITERS,
        scratch_shapes=scratch,
        compiler_params=pltpu.CompilerParams(
            collective_id=0, has_side_effects=True, vmem_limit_bytes=58 << 20
        ),
        name="adjoint",
    )(
        fixed_point,
        upstream,
        norm_gain.reshape(1, width),
        query_weight,
        keyval_weight,
        output_weight,
        log_norm,
        attention_out,
    )
    total = upstream.astype(F32)
    for i in range(ITERS):
        total = total + factors[i] * images[i].astype(F32)
    return total


def solution(mesh, dims=(4, 4, 8)):
    in_specs = (
        P("seq", None),
        P("seq", None),
        P(),
        P(None, "head"),
        P(None, "head"),
        P("head", None),
        P("head", "seq"),
        P("seq", "head"),
    )
    return jax.shard_map(
        functools.partial(shards, dims),
        mesh=mesh,
        in_specs=in_specs,
        out_specs=P("seq", None),
        check_vma=False,
    )
```

```python
import functools

import jax
import jax.numpy as jnp
from jax import lax
from jax.experimental import pallas as pl
from jax.experimental.pallas import tpu as pltpu
from jax.sharding import PartitionSpec as P

WIN = 4
ITERS = 3
GROUP = 4
NORM_EPS = 1e-05
SCALE = 2.0**-12
RESCALE = SCALE**-2
PAIRS = [(i, j) for j in range(ITERS + 1) for i in range(j + 1)]
MIX_EPS = 1e-06
MESH = pl.DeviceIdType.MESH
BF = jnp.bfloat16
F32 = jnp.float32

NT = (((1,), (1,)), ((), ()))


def dot(a, b, dims=(((1,), (0,)), ((), ()))):
    return lax.dot_general(a, b, dims, preferred_element_type=F32)


def kernel(
    dims,
    entries,
    fp_in,
    up_in,
    gain_ref,
    wq_in,
    wkv_in,
    wo_in,
    ln_ref,
    ao_ref,
    xs_out,
    factor_1,
    factor_2,
    factor_3,
    fp,
    wq,
    wo,
    wkv,
    xs,
    kvwin,
    kt_send,
    kt_recv,
    own_kt,
    hid,
    qd,
    dopad,
    ktr,
    sp,
    ao_t,
    gq,
    normed,
    inv,
    krylov,
    gsend,
    gbuf,
    pq_own,
    rs_send,
    rs_recv,
    red_a_send,
    red_a,
    red_b_send,
    red_b,
    red_c_send,
    red_c,
    gram,
    in_sem,
    kv_ssem,
    kv_rsem,
    wkv_ssem,
    wkv_rsem,
    kt_ssem,
    kt_rsem,
    rs_ssem,
    rs_rsem,
    ag_ssem,
    ag_rsem,
    g_ssem,
    g_rsem,
    red_ssem,
    red_rsem,
):
    factor_outs = (factor_1, factor_2, factor_3)
    nx, nz, ny = dims
    blocks = nx * nz * ny
    rows, width = fp.shape
    part = rows // GROUP
    heads = ln_ref.shape[0]
    edge = qd.shape[1] // 2
    span = heads * rows
    s = lax.axis_index("seq")
    h = lax.axis_index("head")
    x = lax.rem(s, nx)
    zh = lax.rem(lax.div(s, nx), nz)
    y = lax.div(s, nx * nz)
    zl = lax.div(h, 2)
    c = lax.rem(h, 2)
    sibling = zl * 2 + (1 - c)
    far = (1 - zl) * 2 + (1 - c)
    across = (1 - zl) * 2 + c
    mine = pl.ds(pl.multiple_of(h * part, part), part)

    def z_peer(d):
        peer = lax.rem(zh * GROUP + h + d, nz * GROUP)
        return (y * nz + lax.div(peer, GROUP)) * nx + x, lax.rem(peer, GROUP)

    def x_peer(d):
        return (y * nz + zh) * nx + lax.rem(x + d, nx), h

    def y_peer(d):
        return (lax.rem(y + d, ny) * nz + zh) * nx + x, h

    def wkv_of(owner):
        lanes = pl.ds(pl.multiple_of(lax.rem(owner, 2) * 2 * edge, 2 * edge), 2 * edge)
        return wkv.at[lax.div(owner, 2), :, lanes]

    loads = [
        pltpu.make_async_copy(fp_in, fp, in_sem.at[0]),
        pltpu.make_async_copy(wkv_in, wkv_of(h), in_sem.at[1]),
        pltpu.make_async_copy(wq_in, wq.at[c], in_sem.at[2]),
        pltpu.make_async_copy(up_in, xs.at[0], in_sem.at[3]),
        pltpu.make_async_copy(wo_in, wo.at[h], in_sem.at[4]),
    ]
    for load in loads:
        load.start()

    kvwin[0:WIN] = jnp.zeros((WIN, rows, 2 * edge), BF)
    kt_recv[...] = jnp.zeros(kt_recv.shape, BF)

    barrier = pltpu.get_barrier_semaphore()

    def greet(device):
        pl.semaphore_signal(barrier, inc=1, device_id=device, device_id_type=MESH)

    for o in range(1, WIN + 1):

        @pl.when(s >= o)
        def _(o=o):
            greet((s - o, h))

        @pl.when(s + o < blocks)
        def _(o=o):
            for q in range(GROUP):
                greet((s + o, q))

    for d in range(1, nz * GROUP):
        greet(z_peer(d))
    for d in range(1, nx):
        greet(x_peer(d))
    for d in range(1, ny):
        greet(y_peer(d))
    greeted = (
        GROUP * jnp.minimum(s, WIN) + jnp.minimum(blocks - 1 - s, WIN)
        + nz * GROUP - 1 + nx - 1 + ny - 1
    )

    gain = gain_ref[...]
    loads[0].wait()
    latent = fp[...].astype(F32)
    inverse = lax.rsqrt(jnp.mean(latent * latent, axis=1, keepdims=True) + NORM_EPS)
    hid[...] = (latent * inverse * gain).astype(BF)
    own_latent = fp[mine, :].astype(F32)
    own_inverse = lax.rsqrt(jnp.mean(own_latent * own_latent, axis=1, keepdims=True) + NORM_EPS)
    inv[...] = jnp.broadcast_to(own_inverse, inv.shape)
    normed[...] = own_latent * own_inverse
    loads[1].wait()
    kvwin[WIN] = dot(hid[...], wkv_of(h)[...]).astype(BF)

    pl.semaphore_wait(barrier, greeted)

    def kv_copy(o):
        return pltpu.make_async_remote_copy(
            src_ref=kvwin.at[WIN],
            dst_ref=kvwin.at[WIN - o],
            send_sem=kv_ssem.at[o - 1],
            recv_sem=kv_rsem.at[o - 1],
            device_id=(s + o, h),
            device_id_type=MESH,
        )

    for o in range(WIN, 0, -1):

        @pl.when(s + o < blocks)
        def _(o=o):
            kv_copy(o).start()

    def wkv_copy(slot, owner, target):
        return pltpu.make_async_remote_copy(
            src_ref=wkv_of(owner),
            dst_ref=wkv_of(owner),
            send_sem=wkv_ssem.at[slot],
            recv_sem=wkv_rsem.at[slot],
            device_id=(s, target),
            device_id_type=MESH,
        )

    wkv_copy(0, h, sibling).start()
    wkv_copy(1, h, across).start()

    loads[2].wait()

    def wq_copy():
        return pltpu.make_async_remote_copy(
            src_ref=wq.at[c],
            dst_ref=wq.at[c],
            send_sem=wkv_ssem.at[3],
            recv_sem=wkv_rsem.at[3],
            device_id=(s, sibling),
            device_id_type=MESH,
        )

    wq_copy().start()
    queries = dot(hid[...], wq[c]).astype(BF)
    zero_half = jnp.zeros((rows, edge), BF)
    for i in range(heads):
        scaled_q = (queries[:, i * edge : (i + 1) * edge].astype(F32) * (edge ** -0.5)).astype(BF)
        qd[i * rows : (i + 1) * rows, :] = jnp.concatenate([scaled_q, zero_half], axis=1)
    ao_t[...] = ao_ref[...].astype(F32).T
    log_row = jnp.concatenate([ln_ref[i : i + 1, :] for i in range(heads)], axis=1)
    dopad[0:edge, :] = jnp.zeros((edge, span), BF)
    qd[span:, 0:edge] = jnp.zeros((span, edge), BF)
    loads[3].wait()
    base_own = xs[0, mine, :].astype(F32)
    krylov[0] = base_own
    krylov[1:ITERS] = jnp.zeros((ITERS - 1,) + base_own.shape, F32)
    loads[4].wait()

    def wo_copy(slot, owner, device):
        return pltpu.make_async_remote_copy(
            src_ref=wo.at[owner],
            dst_ref=wo.at[owner],
            send_sem=wkv_ssem.at[4 + slot],
            recv_sem=wkv_rsem.at[4 + slot],
            device_id=device,
            device_id_type=MESH,
        )

    beside = (y * nz + lax.rem(zh + nz + 2 * zl - 1, nz)) * nx + x
    wo_copy(0, h, (s, sibling)).start()
    wo_copy(1, h, (beside, across)).start()

    def kt_copy(k, o, q):
        return pltpu.make_async_remote_copy(
            src_ref=kt_send.at[k, WIN - o, pl.ds(q * part, part), :],
            dst_ref=kt_recv.at[k, o, h],
            send_sem=kt_ssem.at[k, o],
            recv_sem=kt_rsem.at[k, o],
            device_id=(s - o, q),
            device_id_type=MESH,
        )

    def kt_all(k, o):
        count = GROUP if o > 0 else GROUP - 1
        return pltpu.make_async_remote_copy(
            src_ref=kt_recv.at[k, o, pl.ds(0, count)],
            dst_ref=kt_recv.at[k, o, pl.ds(0, count)],
            send_sem=kt_ssem.at[k, o],
            recv_sem=kt_rsem.at[k, o],
            device_id=(s, sibling),
            device_id_type=MESH,
        )

    def gq_copy(k):
        return pltpu.make_async_remote_copy(
            src_ref=gq.at[k, c],
            dst_ref=gq.at[k, c],
            send_sem=rs_ssem.at[k, 0],
            recv_sem=rs_rsem.at[k, 0],
            device_id=(s, sibling),
            device_id_type=MESH,
        )

    def rs_copy(k, n):
        return pltpu.make_async_remote_copy(
            src_ref=rs_send.at[k, n],
            dst_ref=rs_recv.at[k, n],
            send_sem=rs_ssem.at[k, 1 + n],
            recv_sem=rs_rsem.at[k, 1 + n],
            device_id=(s, across),
            device_id_type=MESH,
        )

    def ag_copy(k, slot, owner, target):
        span = pl.ds(pl.multiple_of(owner * part, part), part)
        return pltpu.make_async_remote_copy(
            src_ref=xs.at[k, span, :],
            dst_ref=xs.at[k, span, :],
            send_sem=ag_ssem.at[k - 1, slot],
            recv_sem=ag_rsem.at[k - 1, slot],
            device_id=(s, target),
            device_id_type=MESH,
        )

    def ag_forward(k):
        ag_copy(k, 1, across, across).wait_recv()
        ag_copy(k, 2, across, sibling).start()

    def ag_finish(k):
        ag_copy(k, 0, sibling, sibling).wait_recv()
        ag_copy(k, 2, sibling, sibling).wait_recv()

    def g_copy(k, target):
        return pltpu.make_async_remote_copy(
            src_ref=gsend.at[k, target],
            dst_ref=gbuf.at[k, mine, :],
            send_sem=g_ssem.at[k],
            recv_sem=g_rsem.at[k],
            device_id=(s, target),
            device_id_type=MESH,
        )

    def g_all(k):
        return pltpu.make_async_remote_copy(
            src_ref=gsend.at[k, pl.ds(0, GROUP - 1)],
            dst_ref=gsend.at[k, pl.ds(0, GROUP - 1)],
            send_sem=g_ssem.at[k],
            recv_sem=g_rsem.at[k],
            device_id=(s, sibling),
            device_id_type=MESH,
        )

    stages = (
        (red_a_send, red_a, nz * GROUP, zh * GROUP + h, z_peer),
        (red_b_send, red_b, nx, x, x_peer),
        (red_c_send, red_c, ny, y, y_peer),
    )

    def red_all(stage):
        send, recv, count, me, peer = stages[stage]
        return pltpu.make_async_remote_copy(
            src_ref=recv.at[pl.ds(0, count - 1)],
            dst_ref=recv.at[pl.ds(0, count - 1)],
            send_sem=red_ssem.at[stage],
            recv_sem=red_rsem.at[stage],
            device_id=peer(1),
            device_id_type=MESH,
        )

    def red_start(stage, value):
        send, recv, count, me, peer = stages[stage]
        send[...] = value
        recv[me] = value
        for d in range(1, count):
            pltpu.make_async_remote_copy(
                src_ref=send,
                dst_ref=recv.at[me],
                send_sem=red_ssem.at[stage],
                recv_sem=red_rsem.at[stage],
                device_id=peer(d),
                device_id_type=MESH,
            ).start()

    def red_finish(stage):
        send, recv, count, me, peer = stages[stage]
        red_all(stage).wait_recv()
        total = recv[0]
        for i in range(1, count):
            total = total + recv[i]
        return total

    group_of_lane = lax.div(lax.broadcasted_iota(jnp.int32, (16, 128), 1), 8)
    row_of = lax.broadcasted_iota(jnp.int32, (16, 128), 0)

    def packed(sums):
        for shift in (64, 32, 16, 8):
            sums = sums + pltpu.roll(sums, shift, 1)
        return jnp.sum(jnp.where(group_of_lane == row_of, sums, 0.0), axis=0, keepdims=True)

    def coefficients(total):
        spread = jnp.where(group_of_lane == row_of, jnp.broadcast_to(total, (16, 128)), 0.0)
        column = jnp.sum(spread, axis=1, keepdims=True)
        index = {pair: i for i, pair in enumerate(PAIRS)}

        def inner(a, b):
            value = 0.0
            for i, left in enumerate(a):
                for j, right in enumerate(b):
                    if left is not None and right is not None:
                        at = index[min(i, j), max(i, j)]
                        value = value + left * right * column[at : at + 1, :]
            return value

        def combined(a, b, factor):
            out = []
            for left, right in zip(a, b):
                if right is None:
                    out.append(left)
                else:
                    out.append(factor * right if left is None else left + factor * right)
            return out

        one = jnp.ones((1, 1), F32)
        base = [one] + [None] * ITERS
        last_image, last_residual, current = base, base, base
        for _ in range(ITERS):
            image = combined(base, [None] + current[:ITERS], 1.0)
            residual = combined(image, current, -1.0)
            change = combined(residual, last_residual, -1.0)
            cross = inner(change, residual) * (RESCALE / entries)
            square = inner(change, change) * (RESCALE / entries)
            mixing = cross / (square + MIX_EPS)
            current = combined(image, combined(image, last_image, -1.0), -mixing)
            last_image, last_residual = image, residual
        return current

    key_pos = lax.broadcasted_iota(jnp.int32, (rows, span), 0)
    query_pos = lax.rem(lax.broadcasted_iota(jnp.int32, (rows, span), 1), rows)

    def probabilities(j):
        block = kvwin[j]
        weights = jnp.exp(dot(block, qd[0:span, :], NT) - log_row)
        if j == 0:
            weights = jnp.where(key_pos > query_pos, weights, 0.0)
        if j == WIN:
            weights = jnp.where(key_pos <= query_pos, weights, 0.0)
        else:
            weights = jnp.where(s >= WIN - j, weights, 0.0)
        sp[j * rows : (j + 1) * rows, span:] = weights.astype(BF)
        ktr[:, j * rows : (j + 1) * rows] = block.astype(F32).T[0:edge, :].astype(BF)

    def spread_cotangents(grad_out, by_rows):
        terms = []
        for i in range(heads):
            entry = slice(i * edge, (i + 1) * edge)
            piece = grad_out[entry, :]
            terms.append(jnp.sum(piece * ao_t[entry, :], axis=0, keepdims=True))
            dopad[edge : 2 * edge, i * rows : (i + 1) * rows] = piece.astype(BF)
            turned = piece.T if by_rows is None else by_rows[:, entry]
            qd[span + i * rows : span + (i + 1) * rows, edge:] = turned.astype(BF)
        return jnp.concatenate(terms, axis=1)

    def block_terms(k, low, high, row_terms):
        count = high - low
        keys = slice(low * rows, high * rows)
        grad_prob = dot(kvwin[low:high].reshape(count * rows, 2 * edge), dopad[...])
        probs = sp[keys, span:]
        sp[keys, :span] = (probs.astype(F32) * (grad_prob - row_terms)).astype(BF)
        key_terms = dot(sp[keys, :], qd[...])
        kt_send[k, low:high] = key_terms.astype(BF).reshape(count, rows, 2 * edge)
        if high == WIN + 1:
            own_kt[...] = key_terms[(count - 1) * rows :]
        for j in range(low, high):
            o = WIN - j
            if o > 0:

                @pl.when(s >= o)
                def _(o=o):
                    for q in range(GROUP):
                        kt_copy(k, o, q).start()

            else:
                for q in range(GROUP):

                    @pl.when(h != q)
                    def _(q=q):
                        kt_copy(k, 0, q).start()

    def lanes(value):
        value = jnp.sum(value, axis=0, keepdims=True)
        total = value[:, 0:128]
        for i in range(1, width // 128):
            total = total + value[:, i * 128 : (i + 1) * 128]
        return total

    def add_inner(newest, count):
        right = krylov[newest] * SCALE
        row = lax.div(newest * (newest + 1), 2)
        for i in range(count):
            gram[pl.ds(row + i, 1), :] = lanes(krylov[i] * SCALE * right)

    def finish(k, first):
        grad_q = dot(ktr[...], sp[:, :span]) * (edge ** -0.5)
        gq[k, c] = (
            jnp.concatenate([grad_q[:, i * rows : (i + 1) * rows] for i in range(heads)], axis=0)
            .T.astype(BF)
        )
        gq_copy(k).start()
        add_inner(jnp.int32(k), ITERS)
        if first:
            wkv_copy(1, across, across).wait_recv()
            wkv_copy(2, across, sibling).start()
            wq_copy().wait_recv()
        gq_copy(k).wait_recv()
        theirs = pl.ds(pl.multiple_of(across * part, part), part)
        for n in range(2):
            half = slice(n * (width // 2), (n + 1) * (width // 2))
            total = jnp.zeros((2 * part, width // 2), F32)
            for i in range(2):
                pair = jnp.concatenate([gq[k, i, theirs, :], gq[k, i, mine, :]], axis=0)
                total = total + dot(pair, wq[i, half, :], NT)
            rs_send[k, n] = total[:part].astype(BF)
            rs_copy(k, n).start()
            pq_own[:, half] = total[part:]

        if not first:
            ag_copy(k, 1, h, across).start()
            ag_copy(k, 0, h, sibling).start()

        for o in range(1, WIN + 1):

            @pl.when(s + o < blocks)
            def _(o=o):
                kt_all(k, o).wait_recv()

        kt_all(k, 0).wait_recv()
        own_terms = own_kt[mine, :]
        collected = []
        for q in range(GROUP):
            total = jnp.where(h == q, own_terms, kt_recv[k, 0, q].astype(F32))
            for o in range(1, WIN + 1):
                total = total + kt_recv[k, o, q].astype(F32)
            collected.append(total.astype(BF))

        if first:
            wkv_copy(0, sibling, sibling).wait_recv()
            wkv_copy(2, sibling, sibling).wait_recv()
            wo_copy(1, across, (s, across)).wait_recv()
            wo_copy(2, across, (s, sibling)).start()

        hidden_grad = pq_own[...]
        for i in range(2):
            pair = jnp.concatenate(collected[2 * i : 2 * i + 2], axis=1)
            hidden_grad = hidden_grad + dot(pair, wkv[i], NT)
        for n in range(2):
            rs_copy(k, n).wait_recv()
        hidden_grad = hidden_grad + jnp.concatenate(
            [rs_recv[k, 0], rs_recv[k, 1]], axis=1
        ).astype(F32)
        scaled = hidden_grad * gain_ref[...]
        own_normed = normed[...]
        mapped = inv[:, 0:1] * (
            scaled - own_normed * jnp.mean(scaled * own_normed, axis=1, keepdims=True)
        )
        vector = mapped.astype(BF)

        def share():
            gsend[k, across] = dot(vector, wo[across], NT)
            g_copy(k, across).start()
            if first:
                wo_copy(2, far, (s, sibling)).wait_recv()
                wo_copy(0, sibling, (s, sibling)).wait_recv()
            gsend[k, far] = dot(vector, wo[far], NT)
            g_copy(k, far).start()
            gsend[k, sibling] = dot(vector, wo[sibling], NT)
            g_copy(k, sibling).start()
            gbuf[k, mine, :] = dot(vector, wo[h], NT)

        if first:
            share()
        else:
            pl.when(k < ITERS - 1)(share)
        xs[k + 1, mine, :] = vector
        krylov[k + 1] = mapped

    row_terms = spread_cotangents(dot(wo[h], xs[0], NT), None)
    for j in range(WIN, -1, -1):
        if j < WIN:

            @pl.when(s >= WIN - j)
            def _(j=j):
                kv_copy(WIN - j).wait_recv()

        probabilities(j)
        block_terms(0, j, j + 1, row_terms)
    gram[...] = jnp.zeros_like(gram)
    finish(0, True)

    def step(k, carry):
        g_all(k - 1).wait_recv()
        by_rows = gbuf[k - 1]
        block_terms(k, 0, WIN + 1, spread_cotangents(by_rows.T, by_rows))
        finish(k, False)
        return carry

    lax.fori_loop(1, ITERS, step, 0)

    ag_copy(ITERS, 1, h, across).start()
    ag_copy(ITERS, 0, h, sibling).start()
    add_inner(jnp.int32(ITERS), ITERS + 1)
    red_start(0, packed(gram[...]))
    for k in range(1, ITERS):
        ag_forward(k)
    for k in range(1, ITERS):
        ag_finish(k)
    older = pltpu.make_async_copy(
        xs.at[pl.ds(0, ITERS)], xs_out.at[pl.ds(0, ITERS)], in_sem.at[5]
    )
    older.start()
    total = red_finish(0)
    red_start(1, total)
    ag_forward(ITERS)
    ag_finish(ITERS)
    newest = pltpu.make_async_copy(xs.at[ITERS], xs_out.at[ITERS], in_sem.at[6])
    newest.start()
    total = red_finish(1)
    red_start(2, total)
    factors = coefficients(red_finish(2))
    for i in range(ITERS):
        factor_outs[i][...] = factors[i + 1]
    older.wait()
    newest.wait()

    for o in range(1, WIN + 1):

        @pl.when(s + o < blocks)
        def _(o=o):
            kv_copy(o).wait_send()

    wkv_copy(0, h, sibling).wait_send()
    wkv_copy(1, h, across).wait_send()
    wkv_copy(2, across, sibling).wait_send()
    wq_copy().wait_send()
    wo_copy(0, h, (s, sibling)).wait_send()
    wo_copy(1, h, (beside, across)).wait_send()
    wo_copy(2, across, (s, sibling)).wait_send()
    for k in range(ITERS - 1):
        g_all(k).wait_send()

    for stage in range(3):
        red_all(stage).wait_send()

    def drain(k, carry):
        for o in range(1, WIN + 1):

            @pl.when(s >= o)
            def _(o=o):
                kt_all(k, o).wait_send()

        kt_all(k, 0).wait_send()
        gq_copy(k).wait_send()
        rs_copy(k, 0).wait_send()
        rs_copy(k, 1).wait_send()
        ag_copy(k + 1, 0, h, sibling).wait_send()
        ag_copy(k + 1, 1, h, across).wait_send()
        ag_copy(k + 1, 2, across, sibling).wait_send()
        return carry

    lax.fori_loop(0, ITERS, drain, 0)


def combine(xs, factor_1, factor_2, factor_3, out, total, sem):
    factors = (factor_1[...], factor_2[...], factor_3[...])
    part = total.shape[0] // GROUP
    copies = []
    for q in range(GROUP):
        here = pl.ds(q * part, part)
        value = xs[0, here, :].astype(F32)
        for i, factor in enumerate(factors):
            value = value + factor * xs[i + 1, here, :].astype(F32)
        total[here, :] = value
        copies.append(pltpu.make_async_copy(total.at[here, :], out.at[here, :], sem.at[q]))
        copies[-1].start()
    for copy in copies:
        copy.wait()


def shards(dims, fixed_point, upstream, norm_gain, query_weight, keyval_weight, output_weight, log_norm, attention_out):
    rows, width = fixed_point.shape
    nx, nz, ny = dims
    heads = log_norm.shape[0]
    cols = query_weight.shape[1]
    kv_cols = keyval_weight.shape[1]
    part = rows // GROUP
    keys = (WIN + 1) * rows
    entries = rows * nx * nz * ny * width
    hbm = pl.BlockSpec(memory_space=pl.ANY)
    vmem = pl.BlockSpec(memory_space=pltpu.VMEM)
    dma = pltpu.SemaphoreType.DMA
    state = pltpu.VMEM((part, width), F32)
    scratch = [
        pltpu.VMEM((rows, width), BF),
        pltpu.VMEM((2, width, cols), BF),
        pltpu.VMEM((GROUP, cols, width), BF),
        pltpu.VMEM((2, width, 2 * kv_cols), BF),
        pltpu.VMEM((ITERS + 1, rows, width), BF),
        pltpu.VMEM((WIN + 1, rows, kv_cols), BF),
        pltpu.VMEM((ITERS, WIN + 1, rows, kv_cols), BF),
        pltpu.VMEM((ITERS, WIN + 1, GROUP, part, kv_cols), BF),
        pltpu.VMEM((rows, kv_cols), F32),
        pltpu.VMEM((rows, width), BF),
        pltpu.VMEM((2 * heads * rows, kv_cols), BF),
        pltpu.VMEM((kv_cols, heads * rows), BF),
        pltpu.VMEM((kv_cols // 2, keys), BF),
        pltpu.VMEM((keys, 2 * heads * rows), BF),
        pltpu.VMEM((cols, rows), F32),
        pltpu.VMEM((ITERS, 2, rows, cols), BF),
        state,
        pltpu.VMEM((part, 128), F32),
        pltpu.VMEM((ITERS + 1, part, width), F32),
        pltpu.VMEM((ITERS - 1, GROUP, part, cols), F32),
        pltpu.VMEM((ITERS - 1, rows, cols), F32),
        state,
        pltpu.VMEM((ITERS, 2, part, width // 2), BF),
        pltpu.VMEM((ITERS, 2, part, width // 2), BF),
        pltpu.VMEM((1, 128), F32),
        pltpu.VMEM((nz * GROUP, 1, 128), F32),
        pltpu.VMEM((1, 128), F32),
        pltpu.VMEM((nx, 1, 128), F32),
        pltpu.VMEM((1, 128), F32),
        pltpu.VMEM((ny, 1, 128), F32),
        pltpu.VMEM((16, 128), F32),
        dma((7,)),
        dma((WIN,)),
        dma((WIN,)),
        dma((7,)),
        dma((7,)),
        dma((ITERS, WIN + 1)),
        dma((ITERS, WIN + 1)),
        dma((ITERS, 3)),
        dma((ITERS, 3)),
        dma((ITERS, 3)),
        dma((ITERS, 3)),
        dma((ITERS - 1,)),
        dma((ITERS - 1,)),
        dma((3,)),
        dma((3,)),
    ]
    images, *factors = pl.pallas_call(
        functools.partial(kernel, dims, float(entries)),
        out_shape=(
            pltpu.VMEM((ITERS + 1, rows, width), BF),
        )
        + (jax.ShapeDtypeStruct((1, 1), F32),) * ITERS,
        in_specs=[hbm, hbm, vmem, hbm, hbm, hbm, vmem, vmem],
        out_specs=(vmem,) + (vmem,) * ITERS,
        scratch_shapes=scratch,
        compiler_params=pltpu.CompilerParams(
            collective_id=0, has_side_effects=True, vmem_limit_bytes=58 << 20
        ),
        name="adjoint",
    )(
        fixed_point,
        upstream,
        norm_gain.reshape(1, width),
        query_weight,
        keyval_weight,
        output_weight,
        log_norm,
        attention_out,
    )
    return pl.pallas_call(
        combine,
        out_shape=jax.ShapeDtypeStruct((rows, width), F32),
        in_specs=[vmem] * (ITERS + 1),
        out_specs=hbm,
        scratch_shapes=[pltpu.VMEM((rows, width), F32), dma((GROUP,))],
        compiler_params=pltpu.CompilerParams(vmem_limit_bytes=8 << 20),
        name="combine",
    )(images, *factors)


def solution(mesh, dims=(4, 4, 8)):
    in_specs = (
        P("seq", None),
        P("seq", None),
        P(),
        P(None, "head"),
        P(None, "head"),
        P("head", None),
        P("head", "seq"),
        P("seq", "head"),
    )
    return jax.shard_map(
        functools.partial(shards, dims),
        mesh=mesh,
        in_specs=in_specs,
        out_specs=P("seq", None),
        check_vma=False,
    )
```

```python
import functools

import jax
import jax.numpy as jnp
from jax import lax
from jax.experimental import pallas as pl
from jax.experimental.pallas import tpu as pltpu
from jax.sharding import PartitionSpec as P

WIN = 4
ITERS = 3
GROUP = 4
NORM_EPS = 1e-05
SCALE = 2.0**-12
RESCALE = SCALE**-2
PAIRS = [(i, j) for j in range(ITERS + 1) for i in range(j + 1)]
MIX_EPS = 1e-06
MESH = pl.DeviceIdType.MESH
BF = jnp.bfloat16
F32 = jnp.float32

NT = (((1,), (1,)), ((), ()))


def dot(a, b, dims=(((1,), (0,)), ((), ()))):
    return lax.dot_general(a, b, dims, preferred_element_type=F32)


def kernel(
    dims,
    entries,
    fp_in,
    up_in,
    gain_ref,
    wq_in,
    wkv_in,
    wo_in,
    ln_ref,
    ao_ref,
    xs_out,
    factors_out,
    fp,
    wq,
    wo,
    wkv,
    xs,
    kvwin,
    kt_send,
    kt_recv,
    own_kt,
    hid,
    qd,
    dopad,
    ktr,
    sp,
    ao_t,
    gq,
    normed,
    inv,
    krylov,
    pq_own,
    rs_send,
    rs_recv,
    red_a_send,
    red_a,
    red_b_send,
    red_b,
    red_c_send,
    red_c,
    gram,
    in_sem,
    kv_ssem,
    kv_rsem,
    wkv_ssem,
    wkv_rsem,
    kt_ssem,
    kt_rsem,
    rs_ssem,
    rs_rsem,
    ag_ssem,
    ag_rsem,
    red_ssem,
    red_rsem,
):
    nx, nz, ny = dims
    blocks = nx * nz * ny
    rows, width = fp.shape
    part = rows // GROUP
    heads = ln_ref.shape[0]
    edge = qd.shape[1] // 2
    span = heads * rows
    s = lax.axis_index("seq")
    h = lax.axis_index("head")
    x = lax.rem(s, nx)
    zh = lax.rem(lax.div(s, nx), nz)
    y = lax.div(s, nx * nz)
    zl = lax.div(h, 2)
    c = lax.rem(h, 2)
    sibling = zl * 2 + (1 - c)
    far = (1 - zl) * 2 + (1 - c)
    across = (1 - zl) * 2 + c
    mine = pl.ds(pl.multiple_of(h * part, part), part)

    def z_peer(d):
        peer = lax.rem(zh * GROUP + h + d, nz * GROUP)
        return (y * nz + lax.div(peer, GROUP)) * nx + x, lax.rem(peer, GROUP)

    def x_peer(d):
        return (y * nz + zh) * nx + lax.rem(x + d, nx), h

    def y_peer(d):
        return (lax.rem(y + d, ny) * nz + zh) * nx + x, h

    def wkv_of(owner):
        lanes = pl.ds(pl.multiple_of(lax.rem(owner, 2) * 2 * edge, 2 * edge), 2 * edge)
        return wkv.at[lax.div(owner, 2), :, lanes]

    loads = [
        pltpu.make_async_copy(fp_in, fp, in_sem.at[0]),
        pltpu.make_async_copy(wkv_in, wkv_of(h), in_sem.at[1]),
        pltpu.make_async_copy(wq_in, wq.at[c], in_sem.at[2]),
        pltpu.make_async_copy(up_in, xs.at[0], in_sem.at[3]),
        pltpu.make_async_copy(wo_in, wo, in_sem.at[4]),
    ]
    for load in loads:
        load.start()

    kvwin[0:WIN] = jnp.zeros((WIN, rows, 2 * edge), BF)
    kt_recv[...] = jnp.zeros(kt_recv.shape, BF)

    barrier = pltpu.get_barrier_semaphore()

    def greet(device):
        pl.semaphore_signal(barrier, inc=1, device_id=device, device_id_type=MESH)

    for o in range(1, WIN + 1):

        @pl.when(s >= o)
        def _(o=o):
            greet((s - o, h))

        @pl.when(s + o < blocks)
        def _(o=o):
            for q in range(GROUP):
                greet((s + o, q))

    for d in range(1, nz * GROUP):
        greet(z_peer(d))
    for d in range(1, nx):
        greet(x_peer(d))
    for d in range(1, ny):
        greet(y_peer(d))
    greeted = (
        GROUP * jnp.minimum(s, WIN) + jnp.minimum(blocks - 1 - s, WIN)
        + nz * GROUP - 1 + nx - 1 + ny - 1
    )

    gain = gain_ref[...]
    loads[0].wait()
    latent = fp[...].astype(F32)
    inverse = lax.rsqrt(jnp.mean(latent * latent, axis=1, keepdims=True) + NORM_EPS)
    hid[...] = (latent * inverse * gain).astype(BF)
    own_latent = fp[mine, :].astype(F32)
    own_inverse = lax.rsqrt(jnp.mean(own_latent * own_latent, axis=1, keepdims=True) + NORM_EPS)
    inv[...] = jnp.broadcast_to(own_inverse, inv.shape)
    normed[...] = own_latent * own_inverse
    loads[1].wait()
    kvwin[WIN] = dot(hid[...], wkv_of(h)[...]).astype(BF)

    pl.semaphore_wait(barrier, greeted)

    def kv_copy(o):
        return pltpu.make_async_remote_copy(
            src_ref=kvwin.at[WIN],
            dst_ref=kvwin.at[WIN - o],
            send_sem=kv_ssem.at[o - 1],
            recv_sem=kv_rsem.at[o - 1],
            device_id=(s + o, h),
            device_id_type=MESH,
        )

    @pl.when(s + WIN < blocks)
    def _():
        kv_copy(WIN).start()

    for o in range(1, WIN):

        @pl.when(x + o < nx)
        def _(o=o):
            kv_copy(o).start()

    def kv_relay(d):
        return pltpu.make_async_remote_copy(
            src_ref=kvwin.at[0],
            dst_ref=kvwin.at[d],
            send_sem=kv_ssem.at[WIN + d - 1],
            recv_sem=kv_rsem.at[WIN - d - 1],
            device_id=(s - d, h),
            device_id_type=MESH,
        )

    def wkv_copy(slot, owner, target):
        return pltpu.make_async_remote_copy(
            src_ref=wkv_of(owner),
            dst_ref=wkv_of(owner),
            send_sem=wkv_ssem.at[slot],
            recv_sem=wkv_rsem.at[slot],
            device_id=(s, target),
            device_id_type=MESH,
        )

    wkv_copy(0, h, sibling).start()
    wkv_copy(1, h, across).start()

    loads[2].wait()

    def wq_copy():
        return pltpu.make_async_remote_copy(
            src_ref=wq.at[c],
            dst_ref=wq.at[c],
            send_sem=wkv_ssem.at[3],
            recv_sem=wkv_rsem.at[3],
            device_id=(s, sibling),
            device_id_type=MESH,
        )

    wq_copy().start()
    queries = dot(hid[...], wq[c]).astype(BF)
    zero_half = jnp.zeros((rows, edge), BF)
    for i in range(heads):
        scaled_q = (queries[:, i * edge : (i + 1) * edge].astype(F32) * (edge ** -0.5)).astype(BF)
        qd[i * rows : (i + 1) * rows, :] = jnp.concatenate([scaled_q, zero_half], axis=1)
    ao_t[...] = ao_ref[...].astype(F32).T
    log_row = jnp.concatenate([ln_ref[i : i + 1, :] for i in range(heads)], axis=1)
    dopad[0:edge, :] = jnp.zeros((edge, span), BF)
    qd[span:, 0:edge] = jnp.zeros((span, edge), BF)
    loads[3].wait()
    base_own = xs[0, mine, :].astype(F32)
    krylov[0] = base_own
    krylov[1:ITERS] = jnp.zeros((ITERS - 1,) + base_own.shape, F32)
    loads[4].wait()

    def kt_copy(k, o, q):
        return pltpu.make_async_remote_copy(
            src_ref=kt_send.at[k, WIN - o, pl.ds(q * part, part), :],
            dst_ref=kt_recv.at[k, o, h],
            send_sem=kt_ssem.at[k, o],
            recv_sem=kt_rsem.at[k, o],
            device_id=(s - o, q),
            device_id_type=MESH,
        )

    def kt_all(k, o):
        count = GROUP if o > 0 else GROUP - 1
        return pltpu.make_async_remote_copy(
            src_ref=kt_recv.at[k, o, pl.ds(0, count)],
            dst_ref=kt_recv.at[k, o, pl.ds(0, count)],
            send_sem=kt_ssem.at[k, o],
            recv_sem=kt_rsem.at[k, o],
            device_id=(s, sibling),
            device_id_type=MESH,
        )

    def gq_copy(k):
        return pltpu.make_async_remote_copy(
            src_ref=gq.at[k, c],
            dst_ref=gq.at[k, c],
            send_sem=rs_ssem.at[k, 0],
            recv_sem=rs_rsem.at[k, 0],
            device_id=(s, sibling),
            device_id_type=MESH,
        )

    def rs_copy(k, n):
        return pltpu.make_async_remote_copy(
            src_ref=rs_send.at[k, n],
            dst_ref=rs_recv.at[k, n],
            send_sem=rs_ssem.at[k, 1 + n],
            recv_sem=rs_rsem.at[k, 1 + n],
            device_id=(s, across),
            device_id_type=MESH,
        )

    def ag_copy(k, slot, owner, target):
        most = width * 3 // 4
        columns = (pl.ds(0, width), pl.ds(0, most), pl.ds(0, most))[slot] if slot < 3 else pl.ds(most, width - most)
        piece = xs.at[k, pl.ds(pl.multiple_of(owner * part, part), part), columns]
        return pltpu.make_async_remote_copy(
            src_ref=piece,
            dst_ref=piece,
            send_sem=ag_ssem.at[k - 1, slot],
            recv_sem=ag_rsem.at[k - 1, slot],
            device_id=(s, target),
            device_id_type=MESH,
        )

    own_slices = ((1, across), (3, far), (4, across), (0, sibling))

    def gathered(k):
        ag_copy(k, 1, across, across).wait_recv()
        ag_copy(k, 2, across, sibling).start()
        ag_copy(k, 0, sibling, sibling).wait_recv()
        ag_copy(k, 4, across, across).wait_recv()
        ag_copy(k, 3, far, far).wait_recv()
        ag_copy(k, 2, far, sibling).wait_recv()

    stages = (
        (red_a_send, red_a, nz * GROUP, zh * GROUP + h, z_peer),
        (red_b_send, red_b, nx, x, x_peer),
        (red_c_send, red_c, ny, y, y_peer),
    )

    def red_all(stage):
        send, recv, count, me, peer = stages[stage]
        return pltpu.make_async_remote_copy(
            src_ref=recv.at[pl.ds(0, count - 1)],
            dst_ref=recv.at[pl.ds(0, count - 1)],
            send_sem=red_ssem.at[stage],
            recv_sem=red_rsem.at[stage],
            device_id=peer(1),
            device_id_type=MESH,
        )

    def red_start(stage, value):
        send, recv, count, me, peer = stages[stage]
        send[...] = value
        recv[me] = value
        for d in range(1, count):
            pltpu.make_async_remote_copy(
                src_ref=send,
                dst_ref=recv.at[me],
                send_sem=red_ssem.at[stage],
                recv_sem=red_rsem.at[stage],
                device_id=peer(d),
                device_id_type=MESH,
            ).start()

    def red_finish(stage):
        send, recv, count, me, peer = stages[stage]
        red_all(stage).wait_recv()
        total = recv[0]
        for i in range(1, count):
            total = total + recv[i]
        return total

    group_of_lane = lax.div(lax.broadcasted_iota(jnp.int32, (16, 128), 1), 8)
    row_of = lax.broadcasted_iota(jnp.int32, (16, 128), 0)

    def packed(sums):
        for shift in (64, 32, 16, 8):
            sums = sums + pltpu.roll(sums, shift, 1)
        return jnp.sum(jnp.where(group_of_lane == row_of, sums, 0.0), axis=0, keepdims=True)

    def coefficients(total):
        spread = jnp.where(group_of_lane == row_of, jnp.broadcast_to(total, (16, 128)), 0.0)
        column = jnp.sum(spread, axis=1, keepdims=True)
        index = {pair: i for i, pair in enumerate(PAIRS)}

        def inner(a, b):
            value = 0.0
            for i, left in enumerate(a):
                for j, right in enumerate(b):
                    if left is not None and right is not None:
                        at = index[min(i, j), max(i, j)]
                        value = value + left * right * column[at : at + 1, :]
            return value

        def combined(a, b, factor):
            out = []
            for left, right in zip(a, b):
                if right is None:
                    out.append(left)
                else:
                    out.append(factor * right if left is None else left + factor * right)
            return out

        one = jnp.ones((1, 1), F32)
        base = [one] + [None] * ITERS
        last_image, last_residual, current = base, base, base
        for _ in range(ITERS):
            image = combined(base, [None] + current[:ITERS], 1.0)
            residual = combined(image, current, -1.0)
            change = combined(residual, last_residual, -1.0)
            cross = inner(change, residual) * (RESCALE / entries)
            square = inner(change, change) * (RESCALE / entries)
            mixing = cross / (square + MIX_EPS)
            current = combined(image, combined(image, last_image, -1.0), -mixing)
            last_image, last_residual = image, residual
        return current

    key_pos = lax.broadcasted_iota(jnp.int32, (rows, span), 0)
    query_pos = lax.rem(lax.broadcasted_iota(jnp.int32, (rows, span), 1), rows)

    def probabilities(j):
        block = kvwin[j]
        weights = jnp.exp(dot(block, qd[0:span, :], NT) - log_row)
        if j == 0:
            weights = jnp.where(key_pos > query_pos, weights, 0.0)
        if j == WIN:
            weights = jnp.where(key_pos <= query_pos, weights, 0.0)
        else:
            weights = jnp.where(s >= WIN - j, weights, 0.0)
        sp[j * rows : (j + 1) * rows, span:] = weights.astype(BF)
        ktr[:, j * rows : (j + 1) * rows] = block.astype(F32).T[0:edge, :].astype(BF)

    def head_cotangents(k):
        grad_out = dot(wo[...], xs[k], NT)
        terms = []
        for i in range(heads):
            piece = grad_out[i * edge : (i + 1) * edge, :]
            terms.append(
                jnp.sum(piece * ao_t[i * edge : (i + 1) * edge, :], axis=0, keepdims=True)
            )
            dopad[edge : 2 * edge, i * rows : (i + 1) * rows] = piece.astype(BF)
            qd[span + i * rows : span + (i + 1) * rows, edge:] = piece.T.astype(BF)
        return jnp.concatenate(terms, axis=1)

    def block_terms(k, low, high, row_terms):
        count = high - low
        keys = slice(low * rows, high * rows)
        grad_prob = dot(kvwin[low:high].reshape(count * rows, 2 * edge), dopad[...])
        probs = sp[keys, span:]
        sp[keys, :span] = (probs.astype(F32) * (grad_prob - row_terms)).astype(BF)
        key_terms = dot(sp[keys, :], qd[...])
        kt_send[k, low:high] = key_terms.astype(BF).reshape(count, rows, 2 * edge)
        if high == WIN + 1:
            own_kt[...] = key_terms[(count - 1) * rows :]
        for j in range(low, high):
            o = WIN - j
            if o > 0:

                @pl.when(s >= o)
                def _(o=o):
                    for q in range(GROUP):
                        kt_copy(k, o, q).start()

            else:
                for q in range(GROUP):

                    @pl.when(h != q)
                    def _(q=q):
                        kt_copy(k, 0, q).start()

    def lanes(value):
        value = jnp.sum(value, axis=0, keepdims=True)
        total = value[:, 0:128]
        for i in range(1, width // 128):
            total = total + value[:, i * 128 : (i + 1) * 128]
        return total

    def add_inner(newest, count):
        right = krylov[newest] * SCALE
        row = lax.div(newest * (newest + 1), 2)
        for i in range(count):
            gram[pl.ds(row + i, 1), :] = lanes(krylov[i] * SCALE * right)

    def finish(k, first):
        grad_q = dot(ktr[...], sp[:, :span]) * (edge ** -0.5)
        gq[k, c] = (
            jnp.concatenate([grad_q[:, i * rows : (i + 1) * rows] for i in range(heads)], axis=0)
            .T.astype(BF)
        )
        gq_copy(k).start()
        add_inner(jnp.int32(k), ITERS)
        if first:
            wkv_copy(1, across, across).wait_recv()
            wkv_copy(2, across, sibling).start()
            wq_copy().wait_recv()
        gq_copy(k).wait_recv()
        theirs = pl.ds(pl.multiple_of(across * part, part), part)
        for n in range(2):
            half = slice(n * (width // 2), (n + 1) * (width // 2))
            total = jnp.zeros((2 * part, width // 2), F32)
            for i in range(2):
                pair = jnp.concatenate([gq[k, i, theirs, :], gq[k, i, mine, :]], axis=0)
                total = total + dot(pair, wq[i, half, :], NT)
            rs_send[k, n] = total[:part].astype(BF)
            rs_copy(k, n).start()
            pq_own[:, half] = total[part:]

        for o in range(1, WIN + 1):

            @pl.when(s + o < blocks)
            def _(o=o):
                kt_all(k, o).wait_recv()

        kt_all(k, 0).wait_recv()
        own_terms = own_kt[mine, :]
        collected = []
        for q in range(GROUP):
            total = jnp.where(h == q, own_terms, kt_recv[k, 0, q].astype(F32))
            for o in range(1, WIN + 1):
                total = total + kt_recv[k, o, q].astype(F32)
            collected.append(total.astype(BF))

        if first:
            wkv_copy(0, sibling, sibling).wait_recv()
            wkv_copy(2, sibling, sibling).wait_recv()

        hidden_grad = pq_own[...]
        for i in range(2):
            pair = jnp.concatenate(collected[2 * i : 2 * i + 2], axis=1)
            hidden_grad = hidden_grad + dot(pair, wkv[i], NT)
        for n in range(2):
            rs_copy(k, n).wait_recv()
        hidden_grad = hidden_grad + jnp.concatenate(
            [rs_recv[k, 0], rs_recv[k, 1]], axis=1
        ).astype(F32)
        scaled = hidden_grad * gain_ref[...]
        own_normed = normed[...]
        mapped = inv[:, 0:1] * (
            scaled - own_normed * jnp.mean(scaled * own_normed, axis=1, keepdims=True)
        )
        xs[k + 1, mine, :] = mapped.astype(BF)
        for slot, target in own_slices:
            ag_copy(k + 1, slot, h, target).start()
        krylov[k + 1] = mapped

    row_terms = head_cotangents(0)
    for j in (WIN, 0, *range(WIN - 1, 0, -1)):
        if j < WIN:

            @pl.when(s >= WIN - j)
            def _(j=j):
                kv_copy(WIN - j).wait_recv()
                if j == 0:
                    for d in range(1, WIN):

                        @pl.when(x >= d)
                        def _(d=d):
                            kv_relay(d).start()

        probabilities(j)
        block_terms(0, j, j + 1, row_terms)
    gram[...] = jnp.zeros_like(gram)
    finish(0, True)

    def step(k, carry):
        gathered(k)
        block_terms(k, 0, WIN + 1, head_cotangents(k))
        finish(k, False)
        return carry

    lax.fori_loop(1, ITERS, step, 0)

    older = pltpu.make_async_copy(
        xs.at[pl.ds(0, ITERS)], xs_out.at[pl.ds(0, ITERS)], in_sem.at[5]
    )
    older.start()
    add_inner(jnp.int32(ITERS), ITERS + 1)
    red_start(0, packed(gram[...]))
    total = red_finish(0)
    red_start(1, total)
    gathered(ITERS)
    newest = pltpu.make_async_copy(xs.at[ITERS], xs_out.at[ITERS], in_sem.at[6])
    newest.start()
    total = red_finish(1)
    red_start(2, total)
    factors = coefficients(red_finish(2))
    for i in range(ITERS):
        factors_out[8 * i : 8 * (i + 1), :] = jnp.broadcast_to(factors[i + 1], (8, 128))
    older.wait()
    newest.wait()

    @pl.when(s + WIN < blocks)
    def _():
        kv_copy(WIN).wait_send()

    for o in range(1, WIN):

        @pl.when(x + o < nx)
        def _(o=o):
            kv_copy(o).wait_send()

        @pl.when((s >= WIN) & (x >= o))
        def _(o=o):
            kv_relay(o).wait_send()

    wkv_copy(0, h, sibling).wait_send()
    wkv_copy(1, h, across).wait_send()
    wkv_copy(2, across, sibling).wait_send()
    wq_copy().wait_send()

    for stage in range(3):
        red_all(stage).wait_send()

    def drain(k, carry):
        for o in range(1, WIN + 1):

            @pl.when(s >= o)
            def _(o=o):
                kt_all(k, o).wait_send()

        kt_all(k, 0).wait_send()
        gq_copy(k).wait_send()
        rs_copy(k, 0).wait_send()
        rs_copy(k, 1).wait_send()
        for slot, target in own_slices:
            ag_copy(k + 1, slot, h, target).wait_send()
        ag_copy(k + 1, 2, across, sibling).wait_send()
        return carry

    lax.fori_loop(0, ITERS, drain, 0)


def combine(xs, factors_in, out, total, sem):
    factors = [factors_in[8 * i : 8 * i + 1, 0:1] for i in range(ITERS)]
    part = total.shape[0] // GROUP
    copies = []
    for q in range(GROUP):
        here = pl.ds(q * part, part)
        value = xs[0, here, :].astype(F32)
        for i, factor in enumerate(factors):
            value = value + factor * xs[i + 1, here, :].astype(F32)
        total[here, :] = value
        copies.append(pltpu.make_async_copy(total.at[here, :], out.at[here, :], sem.at[q]))
        copies[-1].start()
    for copy in copies:
        copy.wait()


def shards(dims, fixed_point, upstream, norm_gain, query_weight, keyval_weight, output_weight, log_norm, attention_out):
    rows, width = fixed_point.shape
    nx, nz, ny = dims
    heads = log_norm.shape[0]
    cols = query_weight.shape[1]
    kv_cols = keyval_weight.shape[1]
    part = rows // GROUP
    keys = (WIN + 1) * rows
    entries = rows * nx * nz * ny * width
    hbm = pl.BlockSpec(memory_space=pl.ANY)
    vmem = pl.BlockSpec(memory_space=pltpu.VMEM)
    dma = pltpu.SemaphoreType.DMA
    state = pltpu.VMEM((part, width), F32)
    scratch = [
        pltpu.VMEM((rows, width), BF),
        pltpu.VMEM((2, width, cols), BF),
        pltpu.VMEM((cols, width), BF),
        pltpu.VMEM((2, width, 2 * kv_cols), BF),
        pltpu.VMEM((ITERS + 1, rows, width), BF),
        pltpu.VMEM((WIN + 1, rows, kv_cols), BF),
        pltpu.VMEM((ITERS, WIN + 1, rows, kv_cols), BF),
        pltpu.VMEM((ITERS, WIN + 1, GROUP, part, kv_cols), BF),
        pltpu.VMEM((rows, kv_cols), F32),
        pltpu.VMEM((rows, width), BF),
        pltpu.VMEM((2 * heads * rows, kv_cols), BF),
        pltpu.VMEM((kv_cols, heads * rows), BF),
        pltpu.VMEM((kv_cols // 2, keys), BF),
        pltpu.VMEM((keys, 2 * heads * rows), BF),
        pltpu.VMEM((cols, rows), F32),
        pltpu.VMEM((ITERS, 2, rows, cols), BF),
        state,
        pltpu.VMEM((part, 128), F32),
        pltpu.VMEM((ITERS + 1, part, width), F32),
        state,
        pltpu.VMEM((ITERS, 2, part, width // 2), BF),
        pltpu.VMEM((ITERS, 2, part, width // 2), BF),
        pltpu.VMEM((1, 128), F32),
        pltpu.VMEM((nz * GROUP, 1, 128), F32),
        pltpu.VMEM((1, 128), F32),
        pltpu.VMEM((nx, 1, 128), F32),
        pltpu.VMEM((1, 128), F32),
        pltpu.VMEM((ny, 1, 128), F32),
        pltpu.VMEM((16, 128), F32),
        dma((7,)),
        dma((2 * WIN - 1,)),
        dma((WIN,)),
        dma((4,)),
        dma((4,)),
        dma((ITERS, WIN + 1)),
        dma((ITERS, WIN + 1)),
        dma((ITERS, 3)),
        dma((ITERS, 3)),
        dma((ITERS, 5)),
        dma((ITERS, 5)),
        dma((3,)),
        dma((3,)),
    ]
    images, factors = pl.pallas_call(
        functools.partial(kernel, dims, float(entries)),
        out_shape=(
            pltpu.VMEM((ITERS + 1, rows, width), BF),
        )
        + (pltpu.VMEM((8 * ITERS, 128), F32),),
        in_specs=[hbm, hbm, vmem, hbm, hbm, hbm, vmem, vmem],
        out_specs=(vmem, vmem),
        scratch_shapes=scratch,
        compiler_params=pltpu.CompilerParams(
            collective_id=0, has_side_effects=True, vmem_limit_bytes=58 << 20
        ),
        name="adjoint",
    )(
        fixed_point,
        upstream,
        norm_gain.reshape(1, width),
        query_weight,
        keyval_weight,
        output_weight,
        log_norm,
        attention_out,
    )
    return pl.pallas_call(
        combine,
        out_shape=jax.ShapeDtypeStruct((rows, width), F32),
        in_specs=[vmem, vmem],
        out_specs=hbm,
        scratch_shapes=[pltpu.VMEM((rows, width), F32), dma((GROUP,))],
        compiler_params=pltpu.CompilerParams(vmem_limit_bytes=8 << 20),
        name="combine",
    )(images, factors)


def solution(mesh, dims=(4, 4, 8)):
    in_specs = (
        P("seq", None),
        P("seq", None),
        P(),
        P(None, "head"),
        P(None, "head"),
        P("head", None),
        P("head", "seq"),
        P("seq", "head"),
    )
    return jax.shard_map(
        functools.partial(shards, dims),
        mesh=mesh,
        in_specs=in_specs,
        out_specs=P("seq", None),
        check_vma=False,
    )
```

```python
import functools

import jax
import jax.numpy as jnp
from jax import lax
from jax.experimental import pallas as pl
from jax.experimental.pallas import tpu as pltpu
from jax.sharding import PartitionSpec as P

WIN = 4
ITERS = 3
GROUP = 4
NORM_EPS = 1e-05
SCALE = 2.0**-12
RESCALE = SCALE**-2
PAIRS = [(i, j) for j in range(ITERS + 1) for i in range(j + 1)]
MIX_EPS = 1e-06
MESH = pl.DeviceIdType.MESH
BF = jnp.bfloat16
F32 = jnp.float32

NT = (((1,), (1,)), ((), ()))


def dot(a, b, dims=(((1,), (0,)), ((), ()))):
    return lax.dot_general(a, b, dims, preferred_element_type=F32)


def kernel(
    dims,
    entries,
    fp_in,
    up_in,
    gain_ref,
    wq_in,
    wkv_in,
    wo_in,
    ln_ref,
    ao_ref,
    xs_out,
    factors_out,
    fp,
    wq,
    wo,
    wkv,
    xs,
    kvwin,
    kt_send,
    kt_recv,
    own_kt,
    hid,
    qd,
    dopad,
    ktr,
    sp,
    ao_t,
    gq,
    normed,
    inv,
    krylov,
    pq_own,
    rs_send,
    rs_recv,
    red_a_send,
    red_a,
    red_b_send,
    red_b,
    red_c_send,
    red_c,
    gram,
    in_sem,
    kv_ssem,
    kv_rsem,
    wkv_ssem,
    wkv_rsem,
    kt_ssem,
    kt_rsem,
    rs_ssem,
    rs_rsem,
    ag_ssem,
    ag_rsem,
    red_ssem,
    red_rsem,
):
    nx, nz, ny = dims
    blocks = nx * nz * ny
    rows, width = fp.shape
    part = rows // GROUP
    heads = ln_ref.shape[0]
    edge = qd.shape[1] // 2
    span = heads * rows
    s = lax.axis_index("seq")
    h = lax.axis_index("head")
    x = lax.rem(s, nx)
    zh = lax.rem(lax.div(s, nx), nz)
    y = lax.div(s, nx * nz)
    zl = lax.div(h, 2)
    c = lax.rem(h, 2)
    sibling = zl * 2 + (1 - c)
    far = (1 - zl) * 2 + (1 - c)
    across = (1 - zl) * 2 + c
    mine = pl.ds(pl.multiple_of(h * part, part), part)

    def z_peer(d):
        peer = lax.rem(zh * GROUP + h + d, nz * GROUP)
        return (y * nz + lax.div(peer, GROUP)) * nx + x, lax.rem(peer, GROUP)

    def x_peer(d):
        return (y * nz + zh) * nx + lax.rem(x + d, nx), h

    def y_peer(d):
        return (lax.rem(y + d, ny) * nz + zh) * nx + x, h

    def wkv_of(owner):
        lanes = pl.ds(pl.multiple_of(lax.rem(owner, 2) * 2 * edge, 2 * edge), 2 * edge)
        return wkv.at[lax.div(owner, 2), :, lanes]

    loads = [
        pltpu.make_async_copy(fp_in, fp, in_sem.at[0]),
        pltpu.make_async_copy(wkv_in, wkv_of(h), in_sem.at[1]),
        pltpu.make_async_copy(wq_in, wq.at[c], in_sem.at[2]),
        pltpu.make_async_copy(up_in, xs.at[0], in_sem.at[3]),
        pltpu.make_async_copy(wo_in, wo, in_sem.at[4]),
    ]
    for load in loads:
        load.start()

    kvwin[0:WIN] = jnp.zeros((WIN, rows, 2 * edge), BF)
    kt_recv[...] = jnp.zeros(kt_recv.shape, BF)

    barrier = pltpu.get_barrier_semaphore()

    def greet(device):
        pl.semaphore_signal(barrier, inc=1, device_id=device, device_id_type=MESH)

    for o in range(1, WIN + 1):

        @pl.when(s >= o)
        def _(o=o):
            greet((s - o, h))

        @pl.when(s + o < blocks)
        def _(o=o):
            for q in range(GROUP):
                greet((s + o, q))

    for d in range(1, nz * GROUP):
        greet(z_peer(d))
    for d in range(1, nx):
        greet(x_peer(d))
    for d in range(1, ny):
        greet(y_peer(d))
    greeted = (
        GROUP * jnp.minimum(s, WIN) + jnp.minimum(blocks - 1 - s, WIN)
        + nz * GROUP - 1 + nx - 1 + ny - 1
    )

    gain = gain_ref[...]
    loads[0].wait()
    latent = fp[...].astype(F32)
    inverse = lax.rsqrt(jnp.mean(latent * latent, axis=1, keepdims=True) + NORM_EPS)
    hid[...] = (latent * inverse * gain).astype(BF)
    own_latent = fp[mine, :].astype(F32)
    own_inverse = lax.rsqrt(jnp.mean(own_latent * own_latent, axis=1, keepdims=True) + NORM_EPS)
    inv[...] = jnp.broadcast_to(own_inverse, inv.shape)
    normed[...] = own_latent * own_inverse
    loads[1].wait()
    kvwin[WIN] = dot(hid[...], wkv_of(h)[...]).astype(BF)

    pl.semaphore_wait(barrier, greeted)

    def kv_copy(o):
        return pltpu.make_async_remote_copy(
            src_ref=kvwin.at[WIN],
            dst_ref=kvwin.at[WIN - o],
            send_sem=kv_ssem.at[o - 1],
            recv_sem=kv_rsem.at[o - 1],
            device_id=(s + o, h),
            device_id_type=MESH,
        )

    @pl.when(s + WIN < blocks)
    def _():
        kv_copy(WIN).start()

    for o in range(1, WIN):

        @pl.when(x + o < nx)
        def _(o=o):
            kv_copy(o).start()

    def kv_relay(d):
        return pltpu.make_async_remote_copy(
            src_ref=kvwin.at[0],
            dst_ref=kvwin.at[d],
            send_sem=kv_ssem.at[WIN + d - 1],
            recv_sem=kv_rsem.at[WIN - d - 1],
            device_id=(s - d, h),
            device_id_type=MESH,
        )

    beside = (y * nz + lax.rem(zh + nz + 2 * zl - 1, nz)) * nx + x

    def wkv_copy(slot, owner, target, block):
        return pltpu.make_async_remote_copy(
            src_ref=wkv_of(owner),
            dst_ref=wkv_of(owner),
            send_sem=wkv_ssem.at[slot],
            recv_sem=wkv_rsem.at[slot],
            device_id=(block, target),
            device_id_type=MESH,
        )


    loads[2].wait()

    def wq_copy():
        return pltpu.make_async_remote_copy(
            src_ref=wq.at[c],
            dst_ref=wq.at[c],
            send_sem=wkv_ssem.at[3],
            recv_sem=wkv_rsem.at[3],
            device_id=(s, sibling),
            device_id_type=MESH,
        )

    wq_copy().start()
    queries = dot(hid[...], wq[c]).astype(BF)
    zero_half = jnp.zeros((rows, edge), BF)
    for i in range(heads):
        scaled_q = (queries[:, i * edge : (i + 1) * edge].astype(F32) * (edge ** -0.5)).astype(BF)
        qd[i * rows : (i + 1) * rows, :] = jnp.concatenate([scaled_q, zero_half], axis=1)
    ao_t[...] = ao_ref[...].astype(F32).T
    log_row = jnp.concatenate([ln_ref[i : i + 1, :] for i in range(heads)], axis=1)
    dopad[0:edge, :] = jnp.zeros((edge, span), BF)
    qd[span:, 0:edge] = jnp.zeros((span, edge), BF)
    loads[3].wait()
    base_own = xs[0, mine, :].astype(F32)
    krylov[0] = base_own
    krylov[1:ITERS] = jnp.zeros((ITERS - 1,) + base_own.shape, F32)
    loads[4].wait()

    def kt_copy(k, o, q):
        return pltpu.make_async_remote_copy(
            src_ref=kt_send.at[k, WIN - o, pl.ds(q * part, part), :],
            dst_ref=kt_recv.at[k, o, h],
            send_sem=kt_ssem.at[k, o],
            recv_sem=kt_rsem.at[k, o],
            device_id=(s - o, q),
            device_id_type=MESH,
        )

    def kt_all(k, o):
        count = GROUP if o > 0 else GROUP - 1
        return pltpu.make_async_remote_copy(
            src_ref=kt_recv.at[k, o, pl.ds(0, count)],
            dst_ref=kt_recv.at[k, o, pl.ds(0, count)],
            send_sem=kt_ssem.at[k, o],
            recv_sem=kt_rsem.at[k, o],
            device_id=(s, sibling),
            device_id_type=MESH,
        )

    def gq_copy(k):
        return pltpu.make_async_remote_copy(
            src_ref=gq.at[k, c],
            dst_ref=gq.at[k, c],
            send_sem=rs_ssem.at[k, 0],
            recv_sem=rs_rsem.at[k, 0],
            device_id=(s, sibling),
            device_id_type=MESH,
        )

    def rs_copy(k, n):
        return pltpu.make_async_remote_copy(
            src_ref=rs_send.at[k, n],
            dst_ref=rs_recv.at[k, n],
            send_sem=rs_ssem.at[k, 1 + n],
            recv_sem=rs_rsem.at[k, 1 + n],
            device_id=(s, across),
            device_id_type=MESH,
        )

    def ag_copy(k, slot, owner, target):
        most = width * 3 // 4
        columns = (pl.ds(0, width), pl.ds(0, most), pl.ds(0, most))[slot] if slot < 3 else pl.ds(most, width - most)
        piece = xs.at[k, pl.ds(pl.multiple_of(owner * part, part), part), columns]
        return pltpu.make_async_remote_copy(
            src_ref=piece,
            dst_ref=piece,
            send_sem=ag_ssem.at[k - 1, slot],
            recv_sem=ag_rsem.at[k - 1, slot],
            device_id=(s, target),
            device_id_type=MESH,
        )

    own_slices = ((1, across), (3, far), (4, across), (0, sibling))

    def gathered(k):
        ag_copy(k, 1, across, across).wait_recv()
        ag_copy(k, 2, across, sibling).start()
        ag_copy(k, 0, sibling, sibling).wait_recv()
        ag_copy(k, 4, across, across).wait_recv()
        ag_copy(k, 3, far, far).wait_recv()
        ag_copy(k, 2, far, sibling).wait_recv()

    stages = (
        (red_c_send, red_c, ny, y, y_peer),
        (red_b_send, red_b, nx, x, x_peer),
        (red_a_send, red_a, nz * GROUP, zh * GROUP + h, z_peer),
    )

    def red_all(stage):
        send, recv, count, me, peer = stages[stage]
        return pltpu.make_async_remote_copy(
            src_ref=recv.at[pl.ds(0, count - 1)],
            dst_ref=recv.at[pl.ds(0, count - 1)],
            send_sem=red_ssem.at[stage],
            recv_sem=red_rsem.at[stage],
            device_id=peer(1),
            device_id_type=MESH,
        )

    def red_start(stage, value):
        send, recv, count, me, peer = stages[stage]
        send[...] = value
        recv[me] = value
        for d in range(1, count):
            pltpu.make_async_remote_copy(
                src_ref=send,
                dst_ref=recv.at[me],
                send_sem=red_ssem.at[stage],
                recv_sem=red_rsem.at[stage],
                device_id=peer(d),
                device_id_type=MESH,
            ).start()

    def red_finish(stage):
        send, recv, count, me, peer = stages[stage]
        red_all(stage).wait_recv()
        total = recv[0]
        for i in range(1, count):
            total = total + recv[i]
        return total

    group_of_lane = lax.div(lax.broadcasted_iota(jnp.int32, (16, 128), 1), 8)
    row_of = lax.broadcasted_iota(jnp.int32, (16, 128), 0)

    def packed(sums):
        for shift in (64, 32, 16, 8):
            sums = sums + pltpu.roll(sums, shift, 1)
        return jnp.sum(jnp.where(group_of_lane == row_of, sums, 0.0), axis=0, keepdims=True)

    def coefficients(total):
        spread = jnp.where(group_of_lane == row_of, jnp.broadcast_to(total, (16, 128)), 0.0)
        column = jnp.sum(spread, axis=1, keepdims=True)
        index = {pair: i for i, pair in enumerate(PAIRS)}

        def inner(a, b):
            value = 0.0
            for i, left in enumerate(a):
                for j, right in enumerate(b):
                    if left is not None and right is not None:
                        at = index[min(i, j), max(i, j)]
                        value = value + left * right * column[at : at + 1, :]
            return value

        def combined(a, b, factor):
            out = []
            for left, right in zip(a, b):
                if right is None:
                    out.append(left)
                else:
                    out.append(factor * right if left is None else left + factor * right)
            return out

        one = jnp.ones((1, 1), F32)
        base = [one] + [None] * ITERS
        last_image, last_residual, current = base, base, base
        for _ in range(ITERS):
            image = combined(base, [None] + current[:ITERS], 1.0)
            residual = combined(image, current, -1.0)
            change = combined(residual, last_residual, -1.0)
            cross = inner(change, residual) * (RESCALE / entries)
            square = inner(change, change) * (RESCALE / entries)
            mixing = cross / (square + MIX_EPS)
            current = combined(image, combined(image, last_image, -1.0), -mixing)
            last_image, last_residual = image, residual
        return current

    key_pos = lax.broadcasted_iota(jnp.int32, (rows, span), 0)
    query_pos = lax.rem(lax.broadcasted_iota(jnp.int32, (rows, span), 1), rows)

    def probabilities(j):
        block = kvwin[j]
        weights = jnp.exp(dot(block, qd[0:span, :], NT) - log_row)
        if j == 0:
            weights = jnp.where(key_pos > query_pos, weights, 0.0)
        if j == WIN:
            weights = jnp.where(key_pos <= query_pos, weights, 0.0)
        else:
            weights = jnp.where(s >= WIN - j, weights, 0.0)
        sp[j * rows : (j + 1) * rows, span:] = weights.astype(BF)
        ktr[:, j * rows : (j + 1) * rows] = block.astype(F32).T[0:edge, :].astype(BF)

    def head_cotangents(k):
        grad_out = dot(wo[...], xs[k], NT)
        terms = []
        for i in range(heads):
            piece = grad_out[i * edge : (i + 1) * edge, :]
            terms.append(
                jnp.sum(piece * ao_t[i * edge : (i + 1) * edge, :], axis=0, keepdims=True)
            )
            dopad[edge : 2 * edge, i * rows : (i + 1) * rows] = piece.astype(BF)
            qd[span + i * rows : span + (i + 1) * rows, edge:] = piece.T.astype(BF)
        return jnp.concatenate(terms, axis=1)

    def block_terms(k, low, high, row_terms):
        count = high - low
        keys = slice(low * rows, high * rows)
        grad_prob = dot(kvwin[low:high].reshape(count * rows, 2 * edge), dopad[...])
        probs = sp[keys, span:]
        sp[keys, :span] = (probs.astype(F32) * (grad_prob - row_terms)).astype(BF)
        key_terms = dot(sp[keys, :], qd[...])
        kt_send[k, low:high] = key_terms.astype(BF).reshape(count, rows, 2 * edge)
        if high == WIN + 1:
            own_kt[...] = key_terms[(count - 1) * rows :]
        for j in range(low, high):
            o = WIN - j
            if o > 0:

                @pl.when(s >= o)
                def _(o=o):
                    for q in range(GROUP):
                        kt_copy(k, o, q).start()

            else:
                for q in range(GROUP):

                    @pl.when(h != q)
                    def _(q=q):
                        kt_copy(k, 0, q).start()

    def lanes(value):
        value = jnp.sum(value, axis=0, keepdims=True)
        total = value[:, 0:128]
        for i in range(1, width // 128):
            total = total + value[:, i * 128 : (i + 1) * 128]
        return total

    def add_inner(newest, count):
        right = krylov[newest] * SCALE
        row = lax.div(newest * (newest + 1), 2)
        for i in range(count):
            gram[pl.ds(row + i, 1), :] = lanes(krylov[i] * SCALE * right)

    def finish(k, first):
        grad_q = dot(ktr[...], sp[:, :span]) * (edge ** -0.5)
        gq[k, c] = (
            jnp.concatenate([grad_q[:, i * rows : (i + 1) * rows] for i in range(heads)], axis=0)
            .T.astype(BF)
        )
        gq_copy(k).start()
        add_inner(jnp.int32(k), ITERS)
        if first:
            wq_copy().wait_recv()
        gq_copy(k).wait_recv()
        theirs = pl.ds(pl.multiple_of(across * part, part), part)
        for n in range(2):
            half = slice(n * (width // 2), (n + 1) * (width // 2))
            total = jnp.zeros((2 * part, width // 2), F32)
            for i in range(2):
                pair = jnp.concatenate([gq[k, i, theirs, :], gq[k, i, mine, :]], axis=0)
                total = total + dot(pair, wq[i, half, :], NT)
            rs_send[k, n] = total[:part].astype(BF)
            rs_copy(k, n).start()
            pq_own[:, half] = total[part:]

        if first:
            wkv_copy(1, across, across, s).wait_recv()
            wkv_copy(2, across, sibling, s).start()

        for o in range(1, WIN + 1):

            @pl.when(s + o < blocks)
            def _(o=o):
                kt_all(k, o).wait_recv()

        kt_all(k, 0).wait_recv()
        own_terms = own_kt[mine, :]
        collected = []
        for q in range(GROUP):
            total = jnp.where(h == q, own_terms, kt_recv[k, 0, q].astype(F32))
            for o in range(1, WIN + 1):
                total = total + kt_recv[k, o, q].astype(F32)
            collected.append(total.astype(BF))

        if first:
            wkv_copy(0, sibling, sibling, s).wait_recv()
            wkv_copy(2, sibling, sibling, s).wait_recv()

        hidden_grad = pq_own[...]
        for i in range(2):
            pair = jnp.concatenate(collected[2 * i : 2 * i + 2], axis=1)
            hidden_grad = hidden_grad + dot(pair, wkv[i], NT)
        for n in range(2):
            rs_copy(k, n).wait_recv()
        hidden_grad = hidden_grad + jnp.concatenate(
            [rs_recv[k, 0], rs_recv[k, 1]], axis=1
        ).astype(F32)
        scaled = hidden_grad * gain_ref[...]
        own_normed = normed[...]
        mapped = inv[:, 0:1] * (
            scaled - own_normed * jnp.mean(scaled * own_normed, axis=1, keepdims=True)
        )
        xs[k + 1, mine, :] = mapped.astype(BF)
        for slot, target in own_slices:
            ag_copy(k + 1, slot, h, target).start()
        krylov[k + 1] = mapped

    row_terms = head_cotangents(0)
    for j in (WIN, 0, *range(WIN - 1, 0, -1)):
        if j < WIN:

            @pl.when(s >= WIN - j)
            def _(j=j):
                kv_copy(WIN - j).wait_recv()
                if j == 0:
                    for d in range(1, WIN):

                        @pl.when(x >= d)
                        def _(d=d):
                            kv_relay(d).start()

        if j == 0:
            wkv_copy(0, h, sibling, s).start()
            wkv_copy(1, h, across, beside).start()
        probabilities(j)
        block_terms(0, j, j + 1, row_terms)
    gram[...] = jnp.zeros_like(gram)
    finish(0, True)

    def step(k, carry):
        gathered(k)
        row_terms = head_cotangents(k)
        block_terms(k, 0, 2, row_terms)
        block_terms(k, 2, WIN + 1, row_terms)
        finish(k, False)
        return carry

    lax.fori_loop(1, ITERS, step, 0)

    older = pltpu.make_async_copy(
        xs.at[pl.ds(0, ITERS)], xs_out.at[pl.ds(0, ITERS)], in_sem.at[5]
    )
    older.start()
    add_inner(jnp.int32(ITERS), ITERS + 1)
    red_start(0, packed(gram[...]))
    total = red_finish(0)
    red_start(1, total)
    gathered(ITERS)
    newest = pltpu.make_async_copy(xs.at[ITERS], xs_out.at[ITERS], in_sem.at[6])
    newest.start()
    total = red_finish(1)
    red_start(2, total)
    factors = coefficients(red_finish(2))
    for i in range(ITERS):
        factors_out[8 * i : 8 * (i + 1), :] = jnp.broadcast_to(factors[i + 1], (8, 128))
    older.wait()
    newest.wait()

    @pl.when(s + WIN < blocks)
    def _():
        kv_copy(WIN).wait_send()

    for o in range(1, WIN):

        @pl.when(x + o < nx)
        def _(o=o):
            kv_copy(o).wait_send()

        @pl.when((s >= WIN) & (x >= o))
        def _(o=o):
            kv_relay(o).wait_send()

    wkv_copy(0, h, sibling, s).wait_send()
    wkv_copy(1, h, across, beside).wait_send()
    wkv_copy(2, across, sibling, s).wait_send()
    wq_copy().wait_send()

    for stage in range(3):
        red_all(stage).wait_send()

    def drain(k, carry):
        for o in range(1, WIN + 1):

            @pl.when(s >= o)
            def _(o=o):
                kt_all(k, o).wait_send()

        kt_all(k, 0).wait_send()
        gq_copy(k).wait_send()
        rs_copy(k, 0).wait_send()
        rs_copy(k, 1).wait_send()
        for slot, target in own_slices:
            ag_copy(k + 1, slot, h, target).wait_send()
        ag_copy(k + 1, 2, across, sibling).wait_send()
        return carry

    lax.fori_loop(0, ITERS, drain, 0)


def combine(xs, factors_in, out, total, sem):
    factors = [factors_in[8 * i : 8 * i + 1, 0:1] for i in range(ITERS)]
    part = total.shape[0] // GROUP
    copies = []
    for q in range(GROUP):
        here = pl.ds(q * part, part)
        value = xs[0, here, :].astype(F32)
        for i, factor in enumerate(factors):
            value = value + factor * xs[i + 1, here, :].astype(F32)
        total[here, :] = value
        copies.append(pltpu.make_async_copy(total.at[here, :], out.at[here, :], sem.at[q]))
        copies[-1].start()
    for copy in copies:
        copy.wait()


def shards(dims, fixed_point, upstream, norm_gain, query_weight, keyval_weight, output_weight, log_norm, attention_out):
    rows, width = fixed_point.shape
    nx, nz, ny = dims
    heads = log_norm.shape[0]
    cols = query_weight.shape[1]
    kv_cols = keyval_weight.shape[1]
    part = rows // GROUP
    keys = (WIN + 1) * rows
    entries = rows * nx * nz * ny * width
    hbm = pl.BlockSpec(memory_space=pl.ANY)
    vmem = pl.BlockSpec(memory_space=pltpu.VMEM)
    dma = pltpu.SemaphoreType.DMA
    state = pltpu.VMEM((part, width), F32)
    scratch = [
        pltpu.VMEM((rows, width), BF),
        pltpu.VMEM((2, width, cols), BF),
        pltpu.VMEM((cols, width), BF),
        pltpu.VMEM((2, width, 2 * kv_cols), BF),
        pltpu.VMEM((ITERS + 1, rows, width), BF),
        pltpu.VMEM((WIN + 1, rows, kv_cols), BF),
        pltpu.VMEM((ITERS, WIN + 1, rows, kv_cols), BF),
        pltpu.VMEM((ITERS, WIN + 1, GROUP, part, kv_cols), BF),
        pltpu.VMEM((rows, kv_cols), F32),
        pltpu.VMEM((rows, width), BF),
        pltpu.VMEM((2 * heads * rows, kv_cols), BF),
        pltpu.VMEM((kv_cols, heads * rows), BF),
        pltpu.VMEM((kv_cols // 2, keys), BF),
        pltpu.VMEM((keys, 2 * heads * rows), BF),
        pltpu.VMEM((cols, rows), F32),
        pltpu.VMEM((ITERS, 2, rows, cols), BF),
        state,
        pltpu.VMEM((part, 128), F32),
        pltpu.VMEM((ITERS + 1, part, width), F32),
        state,
        pltpu.VMEM((ITERS, 2, part, width // 2), BF),
        pltpu.VMEM((ITERS, 2, part, width // 2), BF),
        pltpu.VMEM((1, 128), F32),
        pltpu.VMEM((nz * GROUP, 1, 128), F32),
        pltpu.VMEM((1, 128), F32),
        pltpu.VMEM((nx, 1, 128), F32),
        pltpu.VMEM((1, 128), F32),
        pltpu.VMEM((ny, 1, 128), F32),
        pltpu.VMEM((16, 128), F32),
        dma((7,)),
        dma((2 * WIN - 1,)),
        dma((WIN,)),
        dma((4,)),
        dma((4,)),
        dma((ITERS, WIN + 1)),
        dma((ITERS, WIN + 1)),
        dma((ITERS, 3)),
        dma((ITERS, 3)),
        dma((ITERS, 5)),
        dma((ITERS, 5)),
        dma((3,)),
        dma((3,)),
    ]
    images, factors = pl.pallas_call(
        functools.partial(kernel, dims, float(entries)),
        out_shape=(
            pltpu.VMEM((ITERS + 1, rows, width), BF),
        )
        + (pltpu.VMEM((8 * ITERS, 128), F32),),
        in_specs=[hbm, hbm, vmem, hbm, hbm, hbm, vmem, vmem],
        out_specs=(vmem, vmem),
        scratch_shapes=scratch,
        compiler_params=pltpu.CompilerParams(
            collective_id=0, has_side_effects=True, vmem_limit_bytes=58 << 20
        ),
        name="adjoint",
    )(
        fixed_point,
        upstream,
        norm_gain.reshape(1, width),
        query_weight,
        keyval_weight,
        output_weight,
        log_norm,
        attention_out,
    )
    return pl.pallas_call(
        combine,
        out_shape=jax.ShapeDtypeStruct((rows, width), F32),
        in_specs=[vmem, vmem],
        out_specs=hbm,
        scratch_shapes=[pltpu.VMEM((rows, width), F32), dma((GROUP,))],
        compiler_params=pltpu.CompilerParams(vmem_limit_bytes=8 << 20),
        name="combine",
    )(images, factors)


def solution(mesh, dims=(4, 4, 8)):
    in_specs = (
        P("seq", None),
        P("seq", None),
        P(),
        P(None, "head"),
        P(None, "head"),
        P("head", None),
        P("head", "seq"),
        P("seq", "head"),
    )
    return jax.shard_map(
        functools.partial(shards, dims),
        mesh=mesh,
        in_specs=in_specs,
        out_specs=P("seq", None),
        check_vma=False,
    )
```
